32 devices in a mesh: fsdp: 16 (over z, y, core), tp: 2 (over x).
Axes of the slice: x: 2, y: 2, z: 4, core: 2. Of those that a mesh axis runs over, the one named last changes fastest.
Arguments:
- tokens: bfloat16 [16384, 1024], P(('fsdp', 'tp')), may hold values from -6 to 6
- norm_gains: bfloat16 [2, 1024], P(None, 'fsdp'), may hold values from 0.5 to 1.5
- query_weight: bfloat16 [1024, 1024], P('fsdp', 'tp'), may hold values from -0.1875 to 0.1875
- key_weight: bfloat16 [1024, 1024], P('fsdp', 'tp'), may hold values from -0.1875 to 0.1875
- value_weight: bfloat16 [1024, 1024], P('fsdp', 'tp'), may hold values from -0.1875 to 0.1875
- mix_gate_weight: bfloat16 [1024, 1024], P('fsdp', 'tp'), may hold values from -0.1875 to 0.1875
- output_weight: bfloat16 [1024, 1024], P('tp', 'fsdp'), may hold values from -0.5 to 0.5
- persistent_tokens: bfloat16 [32, 1024], P('fsdp', 'tp'), may hold values from -4 to 4
- memory_init: bfloat16 [1024, 256], P('tp', 'fsdp'), may hold values from -0.5 to 0.5
- gate_weight: bfloat16 [1024, 2816], P('fsdp', 'tp'), may hold values from -0.1875 to 0.1875
- up_weight: bfloat16 [1024, 2816], P('fsdp', 'tp'), may hold values from -0.1875 to 0.1875
- down_weight: bfloat16 [2816, 1024], P('tp', 'fsdp'), may hold values from -0.21875 to 0.21875
- doc_ids: int32 [16384], P('fsdp'), may hold values from 0 to 17, as said below
- span_starts: int32 [256], P('fsdp'), may hold values from 0 to 1, as said below
- memory_rates: float32 [3, 256, 8], P(None, 'fsdp', 'tp'), may hold values from 0.003 to 0.9, as said below
- out_grad: bfloat16 [16384, 1024], P(('fsdp', 'tp')), may hold values from -6 to 6
Outputs:
- output: bfloat16 [16384, 1024], P(('fsdp', 'tp'))
- tokens_grad: bfloat16 [16384, 1024], P(('fsdp', 'tp'))
- norm_gains_grad: float32 [2, 1024], P(None, 'fsdp')
- query_grad: float32 [1024, 1024], P('fsdp', 'tp')
- key_grad: float32 [1024, 1024], P('fsdp', 'tp')
- value_grad: float32 [1024, 1024], P('fsdp', 'tp')
- mix_gate_grad: float32 [1024, 1024], P('fsdp', 'tp')
- output_weight_grad: float32 [1024, 1024], P('tp', 'fsdp')
- persistent_grad: float32 [32, 1024], P('fsdp', 'tp')
- memory_init_grad: float32 [1024, 256], P('tp', 'fsdp')
- gate_grad: float32 [1024, 2816], P('fsdp', 'tp')
- up_grad: float32 [1024, 2816], P('fsdp', 'tp')
- down_grad: float32 [2816, 1024], P('tp', 'fsdp')
The draws below stay inside these ranges and needn't reach their ends.
Inputs may be any that keep to these rules, and one draw needn't show every extreme that they name: `doc_ids`: within each sequence of 1024 tokens the numbers start at 0 and rise by one at each document start; every document but a sequence's last holds 60 to 800 tokens, and one holds exactly 800. Some sequence reaches the largest number that these lengths allow. span_starts[c] is 1 exactly when one of tokens c*64 to c*64 + 63 begins a sequence or has another document number than the token before it; so every sequence's first block has 1. memory_rates[0] holds momenta within 0.3 to 0.9, memory_rates[1] step sizes within 0.003 to 0.03, memory_rates[2] forgetting rates within 0.003 to 0.3.
All inputs are finite; a program needn't handle non-finite values.
Results may differ from the reference program's by a relative error of at most 0.022.
Values may be sent and summed in bfloat16 or wider, within the bound.
No kernel may reach another device: no remote copies, remote signals or barrier semaphores. Data moves between devices by JAX's collectives and lax.ppermute only.
A program may use at most 192 MiB of HBM per device.

```python
import math
import jax
import jax.numpy as jnp
from jax import lax

D = 1024
HEADS = 8
HEAD = 128
FF = 2816
PERSIST = 16
SEQ_LEN = 1024
SPAN = 64
DOC_MIN = 60
DOC_MAX = 800
HH = 1024
TOKENS = 16384


def document_numbers(key):
    folded = jax.random.fold_in(key, 7)
    sequences = TOKENS // SEQ_LEN
    candidates = SEQ_LEN // DOC_MIN + 1
    lengths = jax.random.randint(folded, (sequences, candidates), DOC_MIN, DOC_MAX + 1)
    lengths = lengths.at[0, :].set(DOC_MIN)
    lengths = lengths.at[1, 0].set(DOC_MAX)
    ends = jnp.cumsum(lengths, axis=1)
    places = jnp.arange(SEQ_LEN, dtype=jnp.int32)
    numbers = jnp.sum((ends[:, None, :] <= places[None, :, None]).astype(jnp.int32), axis=2)
    return numbers.reshape(TOKENS).astype(jnp.int32)


def draw_doc_ids(key, part):
    return document_numbers(key)


def draw_span_starts(key, part):
    numbers = document_numbers(key)
    before = jnp.concatenate([jnp.full((1,), -1, jnp.int32), numbers[:-1]])
    places = jnp.arange(TOKENS, dtype=jnp.int32) % SEQ_LEN
    begins = ((numbers != before) | (places == 0)).astype(jnp.int32)
    return jnp.max(begins.reshape(TOKENS // SPAN, SPAN), axis=1).astype(jnp.int32)


def draw_memory_rates(key, part):
    shape = (TOKENS // SPAN, HEADS)
    first = jax.random.uniform(jax.random.fold_in(key, 11), shape, jnp.float32)
    second = jax.random.uniform(jax.random.fold_in(key, 12), shape, jnp.float32)
    third = jax.random.uniform(jax.random.fold_in(key, 13), shape, jnp.float32)
    momentum = 0.3 + 0.6 * first
    stepsize = jnp.exp(math.log(0.003) + second * math.log(10.0))
    forget = jnp.exp(math.log(0.003) + third * math.log(100.0))
    return jnp.stack([momentum, stepsize, forget]).astype(jnp.float32)


def steps_of(own_key, dims, cuts, least, high):
    level = 1.0
    for dim, blocks in cuts:
        heights = jax.random.uniform(jax.random.fold_in(jax.random.fold_in(own_key, 6), dim), (blocks,), jnp.float32, least / len(cuts), high / len(cuts))
        level = level * jnp.repeat(jnp.exp(heights), dims[dim] // blocks).reshape((-1,) + (1,) * (len(dims) - 1 - dim))
    return level


def scatter_about(key, shape, deviation, reach, pieces=(), kind=jnp.bfloat16):
    factor_of = steps_of(key, shape, pieces, -0.22, 0.18) if pieces else 1.0
    array = jax.random.normal(key, shape, jnp.float32) * deviation * factor_of
    return jnp.minimum(jnp.maximum(array, -reach), reach).astype(kind)


def setup_inputs(seed: int = 0) -> dict:
    key_list = jax.random.split(jax.random.key(seed), 17)
    tokens = scatter_about(key_list[0], (TOKENS, D), 1.0, 6.0, ((0, 32),))
    norm_gains = jnp.clip(1.0 + 0.1 * jax.random.normal(key_list[1], (2, D), jnp.float32), 0.5, 1.5).astype(jnp.bfloat16)
    query_weight = scatter_about(key_list[2], (D, HH), D ** -0.5, 0.1875, ((0, 16), (1, 2)))
    key_weight = scatter_about(key_list[3], (D, HH), D ** -0.5, 0.1875, ((0, 16), (1, 2)))
    value_weight = scatter_about(key_list[4], (D, HH), D ** -0.5, 0.1875, ((0, 16), (1, 2)))
    mix_gate_weight = scatter_about(key_list[5], (D, HH), D ** -0.5, 0.1875, ((0, 16), (1, 2)))
    output_weight = scatter_about(key_list[6], (HH, D), HEAD ** -0.5, 0.5, ((0, 2), (1, 16)))
    persistent_tokens = scatter_about(key_list[7], (2 * PERSIST, HH), 1.0, 4.0, ((0, 16), (1, 2)))
    memory_init = scatter_about(key_list[8], (HH, 2 * HEAD), HEAD ** -0.5, 0.5, ((0, 2), (1, 16)))
    gate_weight = scatter_about(key_list[9], (D, FF), D ** -0.5, 0.1875, ((0, 16), (1, 2)))
    up_weight = scatter_about(key_list[10], (D, FF), D ** -0.5, 0.1875, ((0, 16), (1, 2)))
    down_weight = scatter_about(key_list[11], (FF, D), (FF // 4) ** -0.5, 0.21875, ((0, 2), (1, 16)))
    doc_ids = draw_doc_ids(jax.random.fold_in(key_list[16], 71), 0)
    span_starts = draw_span_starts(jax.random.fold_in(key_list[16], 71), 0)
    memory_rates = draw_memory_rates(jax.random.fold_in(key_list[16], 71), 0)
    out_grad = scatter_about(key_list[15], (TOKENS, D), 1.0, 6.0, ((0, 32),))
    return dict(tokens=tokens, norm_gains=norm_gains, query_weight=query_weight, key_weight=key_weight, value_weight=value_weight, mix_gate_weight=mix_gate_weight, output_weight=output_weight, persistent_tokens=persistent_tokens, memory_init=memory_init, gate_weight=gate_weight, up_weight=up_weight, down_weight=down_weight, doc_ids=doc_ids, span_starts=span_starts, memory_rates=memory_rates, out_grad=out_grad)


EPSILON = 1e-05
MASKED_SCORE = -1e+30

@jax.custom_vjp
def low(v):
    return lax.optimization_barrier(v.astype(jnp.bfloat16)).astype(jnp.float32)

@jax.custom_vjp
def low_back(v):
    return v

def low_keep(v):
    return (low(v), None)

def low_pass(kept, grad):
    return (grad,)

def back_keep(v):
    return (v, None)

def back_low(kept, grad):
    return (low(grad),)
low.defvjp(low_keep, low_pass)
low_back.defvjp(back_keep, back_low)

def product(left, right):
    return jnp.dot(left, right, precision=lax.Precision.HIGHEST)

def einsum_high(form, left, right):
    return jnp.einsum(form, left, right, precision=lax.Precision.HIGHEST)

def rms_norm(values, gain):
    return values * lax.rsqrt(lax.optimization_barrier(jnp.mean(values * values, axis=-1, keepdims=True)) + EPSILON) * gain

def memory_head(queries, key_rows, value_rows, documents, starts, rate_rows, init_one, init_two):
    spans = starts.shape[0]
    query_blocks = queries.reshape(spans, SPAN, HEAD)
    key_blocks = key_rows.reshape(spans, SPAN, HEAD)
    value_blocks = value_rows.reshape(spans, SPAN, HEAD)
    doc_blocks = documents.reshape(spans, SPAN)
    live_rows = (doc_blocks == doc_blocks[:, SPAN - 1:SPAN]).astype(jnp.float32) / SPAN
    resets = starts.astype(jnp.float32)

    def advance(state, inputs):
        weight_one, weight_two, moment_one, moment_two = state
        query_block, key_block, value_block, live_block, reset_now, momentum, stepsize, forget = inputs
        weight_one = (1.0 - reset_now) * weight_one + reset_now * init_one
        weight_two = (1.0 - reset_now) * weight_two + reset_now * init_two
        moment_one = (1.0 - reset_now) * moment_one
        moment_two = (1.0 - reset_now) * moment_two
        readout = product(jax.nn.silu(product(query_block, weight_one)), weight_two)
        hidden = product(key_block, weight_one)
        sigmoid_h = jax.nn.sigmoid(hidden)
        active = hidden * sigmoid_h
        errors = (product(active, weight_two) - value_block) * live_block[:, None]
        grad_two = product(active.T, errors)
        grad_one = product(key_block.T, product(errors, weight_two.T) * (sigmoid_h * (1.0 + hidden * (1.0 - sigmoid_h))))
        moment_one = momentum * moment_one - stepsize * grad_one
        moment_two = momentum * moment_two - stepsize * grad_two
        weight_one = (1.0 - forget) * weight_one + moment_one
        weight_two = (1.0 - forget) * weight_two + moment_two
        return ((weight_one, weight_two, moment_one, moment_two), readout)
    zero_state = jnp.zeros((HEAD, HEAD), jnp.float32)
    finals, readout = lax.scan(jax.checkpoint(advance), (init_one, init_two, zero_state, zero_state), (query_blocks, key_blocks, value_blocks, live_rows, resets, rate_rows[0], rate_rows[1], rate_rows[2]))
    return readout.reshape(spans * SPAN, HEAD)

def memory_all(queries, key_rows, value_rows, memory_init, documents, starts, rate_rows):
    sequences = documents.shape[0] // SEQ_LEN
    head_count = queries.shape[1] // HEAD

    def by_head(values):
        return values.reshape(sequences, SEQ_LEN, head_count, HEAD).transpose(0, 2, 1, 3)
    weight_one = memory_init[:, :HEAD].reshape(head_count, HEAD, HEAD)
    weight_two = memory_init[:, HEAD:].reshape(head_count, HEAD, HEAD)
    per_rates = rate_rows.reshape(3, sequences, -1, head_count).transpose(1, 3, 0, 2)
    per_head = jax.vmap(memory_head, in_axes=(0, 0, 0, None, None, 0, 0, 0))
    per_sequence = jax.vmap(per_head, in_axes=(0, 0, 0, 0, 0, 0, None, None))
    readout = per_sequence(by_head(queries), by_head(key_rows), by_head(value_rows), documents.reshape(sequences, SEQ_LEN), starts.reshape(sequences, -1), per_rates, weight_one, weight_two)
    return readout.transpose(0, 2, 1, 3).reshape(sequences * SEQ_LEN, head_count * HEAD)

def attention(queries, key_rows, value_rows, fixed_keys, fixed_values, documents):
    scaling = HEAD ** (-0.5)
    scores = low_back(einsum_high('qhd,khd->hqk', queries, key_rows) * scaling)
    fixed_scores = low_back(einsum_high('qhd,phd->hqp', queries, fixed_keys) * scaling)
    places = jnp.arange(SEQ_LEN)
    allowed = (documents[:, None] == documents[None, :]) & (places[None, :] <= places[:, None])
    scores = jnp.where(allowed[None], scores, MASKED_SCORE)
    joined = jnp.concatenate([fixed_scores, scores], axis=2)
    highest = lax.optimization_barrier(jnp.max(joined, axis=2, keepdims=True))
    weights = jnp.exp(joined - highest)
    probability = low(weights / lax.optimization_barrier(jnp.sum(weights, axis=2, keepdims=True)))
    result = einsum_high('hqp,phd->qhd', probability[:, :, :PERSIST], fixed_values)
    result = result + einsum_high('hqk,khd->qhd', probability[:, :, PERSIST:], value_rows)
    return low_back(result)

def group_forward(rows_in, documents, starts, rate_rows, params):
    gains, query_weight, key_weight, value_weight, mix_gate_weight, output_weight, persistent_tokens, memory_init, gate_weight, up_weight, down_weight = params
    normed = low(rms_norm(rows_in, gains[0]))
    queries = low_back(low(product(normed, query_weight)))
    key_rows = low_back(low(product(normed, key_weight)))
    value_rows = low_back(low(product(normed, value_weight)))
    gate_pre = low_back(product(normed, mix_gate_weight))
    sequences = documents.shape[0] // SEQ_LEN

    def by_head(values):
        return values.reshape(sequences, SEQ_LEN, HEADS, HEAD)
    fixed_keys = persistent_tokens[:PERSIST].reshape(PERSIST, HEADS, HEAD)
    fixed_values = persistent_tokens[PERSIST:].reshape(PERSIST, HEADS, HEAD)

    def one_sequence(inputs):
        return attention(inputs[0], inputs[1], inputs[2], fixed_keys, fixed_values, inputs[3])
    attended = lax.map(jax.checkpoint(one_sequence), (by_head(queries), by_head(key_rows), by_head(value_rows), documents.reshape(sequences, SEQ_LEN)))
    attended = attended.reshape(sequences * SEQ_LEN, HEADS * HEAD)
    recalled = memory_all(queries, key_rows, value_rows, memory_init, documents, starts, rate_rows)
    combined = low(attended + jax.nn.sigmoid(gate_pre) * recalled)
    hidden_one = rows_in + low_back(product(combined, output_weight))
    normed_two = low(rms_norm(hidden_one, gains[1]))
    gate_rows = low_back(product(normed_two, gate_weight))
    up_rows = low_back(product(normed_two, up_weight))
    hidden = low(jax.nn.silu(gate_rows) * up_rows)
    return hidden_one + product(hidden, down_weight)

def reference(tokens, norm_gains, query_weight, key_weight, value_weight, mix_gate_weight, output_weight, persistent_tokens, memory_init, gate_weight, up_weight, down_weight, doc_ids, span_starts, memory_rates, out_grad):
    sequences = TOKENS // SEQ_LEN
    per_group = 4 if sequences % 4 == 0 else 1
    groups = sequences // per_group
    group_rows = per_group * SEQ_LEN
    doc_groups = doc_ids.reshape(groups, group_rows)
    start_groups = span_starts.reshape(groups, group_rows // SPAN)
    rate_groups = memory_rates.reshape(3, groups, group_rows // SPAN, HEADS).transpose(1, 0, 2, 3)
    weight_list = [norm_gains.astype(jnp.float32), query_weight.astype(jnp.float32), key_weight.astype(jnp.float32), value_weight.astype(jnp.float32), mix_gate_weight.astype(jnp.float32), output_weight.astype(jnp.float32), persistent_tokens.astype(jnp.float32), memory_init.astype(jnp.float32), gate_weight.astype(jnp.float32), up_weight.astype(jnp.float32), down_weight.astype(jnp.float32)]

    def layer_all(rows_all, *params):

        def run_group(inputs):
            return group_forward(inputs[0], inputs[1], inputs[2], inputs[3], params)
        outputs = lax.map(jax.checkpoint(run_group), (rows_all.reshape(groups, group_rows, D), doc_groups, start_groups, rate_groups))
        return outputs.reshape(TOKENS, D)
    result, pullback = jax.vjp(layer_all, tokens.astype(jnp.float32), *weight_list)
    gradients = pullback(out_grad.astype(jnp.float32))
    return (result.astype(jnp.bfloat16), gradients[0].astype(jnp.bfloat16), gradients[1], gradients[2], gradients[3], gradients[4], gradients[5], gradients[6], gradients[7], gradients[8], gradients[9], gradients[10], gradients[11])
```

```python
import functools
import jax, jax.numpy as jnp
from jax import lax
from jax.experimental import pallas as pl
from jax.experimental.pallas import tpu as pltpu
from jax.sharding import PartitionSpec as P

HEAD = 128
SPAN = 64
SEQ_LEN = 1024
BF16 = jnp.bfloat16
F32 = jnp.float32
NN = (((1,), (0,)), ((), ()))
NT = (((1,), (1,)), ((), ()))
TN = (((0,), (0,)), ((), ()))


def dot(left, right, dims=NN):
    return lax.dot_general(left, right, dims, preferred_element_type=F32)


def sigmoid(values):
    return 0.5 * jnp.tanh(0.5 * values) + 0.5


def memory_forward_kernel(
    unroll, sequences, heads, starts_ref, rates_ref, queries_ref, keys_ref, values_ref, live_ref,
    init_ref, recalled_ref, states_ref, first_ref, second_ref, moment_one_ref, moment_two_ref,
):
    spans = SEQ_LEN // SPAN
    step = pl.program_id(0)
    chains = [(s, h) for s in range(sequences) for h in range(heads)]

    @pl.when(step == 0)
    def _():
        for place, (s, h) in enumerate(chains):
            first_ref[place] = jnp.zeros((HEAD, HEAD), F32)
            second_ref[place] = jnp.zeros((HEAD, HEAD), F32)
            moment_one_ref[place] = jnp.zeros((HEAD, HEAD), F32)
            moment_two_ref[place] = jnp.zeros((HEAD, HEAD), F32)

    state = [
        (first_ref[i], second_ref[i], moment_one_ref[i], moment_two_ref[i])
        for i in range(len(chains))
    ]
    for part in range(unroll):
        rows = pl.ds(part * SPAN, SPAN)
        span = step * unroll + part
        begins = [starts_ref[s * spans + span] != 0 for s in range(sequences)]
        used = []
        for place, (s, h) in enumerate(chains):
            one, two, moment_one, moment_two = state[place]
            start = init_ref[pl.ds(h * HEAD, HEAD), :]
            used.append(
                (
                    jnp.where(begins[s], start[:, :HEAD], one),
                    jnp.where(begins[s], start[:, HEAD:], two),
                    jnp.where(begins[s], 0.0, moment_one),
                    jnp.where(begins[s], 0.0, moment_two),
                )
            )
        low = [(one.astype(BF16), two.astype(BF16)) for one, two, _, _ in used]
        for place in range(len(chains)):
            states_ref[part, place, :, :HEAD] = low[place][0]
            states_ref[part, place, :, HEAD:] = low[place][1]
        cols = [pl.ds(h * HEAD, HEAD) for _, h in chains]
        keys = [keys_ref[s, rows, cols[i]] for i, (s, _) in enumerate(chains)]
        hidden = [dot(keys[i], low[i][0]) for i in range(len(chains))]
        gates = [sigmoid(value) for value in hidden]
        active = [(h * g).astype(BF16) for h, g in zip(hidden, gates)]
        outs = [dot(active[i], low[i][1]) for i in range(len(chains))]
        errors = [
            ((outs[i] - values_ref[s, rows, cols[i]].astype(F32)) * live_ref[s, rows, :]).astype(BF16)
            for i, (s, _) in enumerate(chains)
        ]
        back = [dot(errors[i], low[i][1], NT) for i in range(len(chains))]
        inner = [
            (b * (g * (1.0 + h * (1.0 - g)))).astype(BF16)
            for b, h, g in zip(back, hidden, gates)
        ]
        grad_one = [dot(keys[i], inner[i], TN) for i in range(len(chains))]
        grad_two = [dot(active[i], errors[i], TN) for i in range(len(chains))]
        state = []
        for place, (s, h) in enumerate(chains):
            one, two, moment_one, moment_two = used[place]
            index = (s * spans + span) * heads + h
            stride = sequences * spans * heads
            momentum = rates_ref[index]
            size = rates_ref[stride + index]
            keep = 1.0 - rates_ref[2 * stride + index]
            moment_one = momentum * moment_one - size * grad_one[place]
            moment_two = momentum * moment_two - size * grad_two[place]
            state.append((keep * one + moment_one, keep * two + moment_two, moment_one, moment_two))
        for place, (s, h) in enumerate(chains):
            asked = dot(queries_ref[s, rows, cols[place]], low[place][0])
            asked = (asked * sigmoid(asked)).astype(BF16)
            recalled_ref[s, rows, cols[place]] = dot(asked, low[place][1]).astype(recalled_ref.dtype)
    for place in range(len(chains)):
        first_ref[place], second_ref[place], moment_one_ref[place], moment_two_ref[place] = state[place]


def memory_forward(queries, key_rows, value_rows, live, starts, rates, init, unroll=2):
    rows, width = queries.shape
    sequences, heads = rows // SEQ_LEN, width // HEAD
    spans = SEQ_LEN // SPAN
    chains = sequences * heads

    def by_seq(values):
        return values.reshape(sequences, SEQ_LEN, width)

    block = pl.BlockSpec((sequences, unroll * SPAN, width), lambda c: (0, c, 0))
    smem = pl.BlockSpec(memory_space=pltpu.SMEM)
    recalled, states = pl.pallas_call(
        functools.partial(memory_forward_kernel, unroll, sequences, heads),
        grid=(spans // unroll,),
        in_specs=[
            smem, smem, block, block, block,
            pl.BlockSpec((sequences, unroll * SPAN, 1), lambda c: (0, c, 0)),
            pl.BlockSpec((heads * HEAD, 2 * HEAD), lambda c: (0, 0)),
        ],
        out_specs=[
            block,
            pl.BlockSpec((unroll, chains, HEAD, 2 * HEAD), lambda c: (c, 0, 0, 0)),
        ],
        out_shape=[
            jax.ShapeDtypeStruct((sequences, SEQ_LEN, width), F32),
            jax.ShapeDtypeStruct((spans, chains, HEAD, 2 * HEAD), BF16),
        ],
        scratch_shapes=[pltpu.VMEM((chains, HEAD, HEAD), F32)] * 4,
        name="memory_forward",
    )(
        starts, rates.reshape(-1), by_seq(queries), by_seq(key_rows), by_seq(value_rows),
        live.reshape(sequences, SEQ_LEN, 1), init,
    )
    return recalled.reshape(rows, width), states


def memory_backward_kernel(
    unroll, sequences, heads, starts_ref, rates_ref, queries_ref, keys_ref, values_ref, live_ref,
    grads_ref, states_ref, query_out, key_out, value_out, init_out,
    first_ref, second_ref, moment_one_ref, moment_two_ref, total_ref,
):
    spans = SEQ_LEN // SPAN
    step = pl.program_id(0)
    chains = [(s, h) for s in range(sequences) for h in range(heads)]
    count = len(chains)
    zero = jnp.zeros((HEAD, HEAD), F32)

    @pl.when(step == 0)
    def _():
        for i in range(count):
            first_ref[i] = zero
            second_ref[i] = zero
            moment_one_ref[i] = zero
            moment_two_ref[i] = zero
            total_ref[i] = jnp.zeros((HEAD, 2 * HEAD), F32)

    state = [(first_ref[i], second_ref[i], moment_one_ref[i], moment_two_ref[i]) for i in range(count)]
    cols = [pl.ds(h * HEAD, HEAD) for _, h in chains]
    for part in reversed(range(unroll)):
        rows = pl.ds(part * SPAN, SPAN)
        span = spans - (step + 1) * unroll + part
        stride = sequences * spans * heads
        each = range(count)
        one = [states_ref[part, i, :, :HEAD] for i in each]
        two = [states_ref[part, i, :, HEAD:] for i in each]
        queries = [queries_ref[chains[i][0], rows, cols[i]] for i in each]
        keys = [keys_ref[chains[i][0], rows, cols[i]] for i in each]
        values = [values_ref[chains[i][0], rows, cols[i]].astype(F32) for i in each]
        live = [live_ref[chains[i][0], rows, :] for i in each]
        grads = [grads_ref[chains[i][0], rows, cols[i]].astype(BF16) for i in each]
        hidden = [dot(keys[i], one[i]) for i in each]
        gates = [sigmoid(hidden[i]) for i in each]
        active = [(hidden[i] * gates[i]).astype(BF16) for i in each]
        errors = [((dot(active[i], two[i]) - values[i]) * live[i]).astype(BF16) for i in each]
        back = [dot(errors[i], two[i], NT) for i in each]
        slope = [gates[i] * (1.0 + hidden[i] * (1.0 - gates[i])) for i in each]
        bend = [
            gates[i] * (1.0 - gates[i]) * (2.0 + hidden[i] * (1.0 - 2.0 * gates[i])) * back[i]
            for i in each
        ]
        inner = [(back[i] * slope[i]).astype(BF16) for i in each]
        asked = [dot(queries[i], one[i]) for i in each]
        asked_gate = [sigmoid(asked[i]) for i in each]
        asked_active = [(asked[i] * asked_gate[i]).astype(BF16) for i in each]
        asked_grad = [
            (
                dot(grads[i], two[i], NT)
                * (asked_gate[i] * (1.0 + asked[i] * (1.0 - asked_gate[i])))
            ).astype(BF16)
            for i in each
        ]
        for i in each:
            query_out[chains[i][0], rows, cols[i]] = dot(asked_grad[i], one[i], NT)
        momentum, size, keep = [], [], []
        for s, h in chains:
            index = (s * spans + span) * heads + h
            momentum.append(rates_ref[index])
            size.append(rates_ref[stride + index])
            keep.append(1.0 - rates_ref[2 * stride + index])
        sum_one = [state[i][0] + state[i][2] for i in each]
        sum_two = [state[i][1] + state[i][3] for i in each]
        step_one = [(-size[i] * sum_one[i]).astype(BF16) for i in each]
        step_two = [(-size[i] * sum_two[i]).astype(BF16) for i in each]
        inner_grad = [dot(keys[i], step_one[i]) for i in each]
        back_grad = [(inner_grad[i] * slope[i]).astype(BF16) for i in each]
        error_grad = [
            (dot(back_grad[i], two[i]) + dot(active[i], step_two[i])) * live[i] for i in each
        ]
        for i in each:
            value_out[chains[i][0], rows, cols[i]] = -error_grad[i]
        out_grad = [error_grad[i].astype(BF16) for i in each]
        active_grad = [dot(errors[i], step_two[i], NT) + dot(out_grad[i], two[i], NT) for i in each]
        hidden_grad = [
            (active_grad[i] * slope[i] + inner_grad[i] * bend[i]).astype(BF16) for i in each
        ]
        new_one = [
            keep[i] * state[i][0] + dot(keys[i], hidden_grad[i], TN) + dot(queries[i], asked_grad[i], TN)
            for i in each
        ]
        new_two = [
            keep[i] * state[i][1]
            + dot(back_grad[i], errors[i], TN)
            + dot(active[i], out_grad[i], TN)
            + dot(asked_active[i], grads[i], TN)
            for i in each
        ]
        for i in each:
            key_out[chains[i][0], rows, cols[i]] = dot(inner[i], step_one[i], NT) + dot(
                hidden_grad[i], one[i], NT
            )
        begins = [starts_ref[s * spans + span] != 0 for s in range(sequences)]
        state = []
        for i, (s, h) in enumerate(chains):
            begin = begins[s]
            total_ref[i, :, :HEAD] += jnp.where(begin, new_one[i], 0.0)
            total_ref[i, :, HEAD:] += jnp.where(begin, new_two[i], 0.0)
            state.append(
                (
                    jnp.where(begin, 0.0, new_one[i]),
                    jnp.where(begin, 0.0, new_two[i]),
                    jnp.where(begin, 0.0, momentum[i] * sum_one[i]),
                    jnp.where(begin, 0.0, momentum[i] * sum_two[i]),
                )
            )
    for i in range(count):
        first_ref[i], second_ref[i], moment_one_ref[i], moment_two_ref[i] = state[i]

    @pl.when(step == pl.num_programs(0) - 1)
    def _():
        for h in range(heads):
            init_out[pl.ds(h * HEAD, HEAD), :] = sum(
                total_ref[s * heads + h] for s in range(sequences)
            )


def memory_backward(
    queries, key_rows, value_rows, live, starts, rates, grads, states, unroll=2
):
    rows, width = queries.shape
    sequences, heads = rows // SEQ_LEN, width // HEAD
    spans = SEQ_LEN // SPAN
    chains = sequences * heads
    steps = spans // unroll

    def by_seq(values):
        return values.reshape(sequences, SEQ_LEN, width)

    block = pl.BlockSpec((sequences, unroll * SPAN, width), lambda c: (0, steps - 1 - c, 0))
    smem = pl.BlockSpec(memory_space=pltpu.SMEM)
    shape = jax.ShapeDtypeStruct((sequences, SEQ_LEN, width), F32)
    query_mem, key_mem, value_mem, init_grad = pl.pallas_call(
        functools.partial(memory_backward_kernel, unroll, sequences, heads),
        grid=(steps,),
        in_specs=[
            smem, smem, block, block, block,
            pl.BlockSpec((sequences, unroll * SPAN, 1), lambda c: (0, steps - 1 - c, 0)),
            block,
            pl.BlockSpec((unroll, chains, HEAD, 2 * HEAD), lambda c: (steps - 1 - c, 0, 0, 0)),
        ],
        out_specs=[
            block, block, block,
            pl.BlockSpec((heads * HEAD, 2 * HEAD), lambda c: (0, 0)),
        ],
        out_shape=[
            shape, shape, shape,
            jax.ShapeDtypeStruct((heads * HEAD, 2 * HEAD), F32),
        ],
        scratch_shapes=[pltpu.VMEM((chains, HEAD, HEAD), F32)] * 4
        + [pltpu.VMEM((chains, HEAD, 2 * HEAD), F32)],
        name="memory_backward",
    )(
        starts, rates.reshape(-1), by_seq(queries), by_seq(key_rows), by_seq(value_rows),
        live.reshape(sequences, SEQ_LEN, 1), by_seq(grads), states,
    )
    return tuple(x.reshape(rows, width) for x in (query_mem, key_mem, value_mem)) + (init_grad,)

PERSIST = 16
TILE = 256
MASKED_SCORE = -1e30
SCALING = HEAD ** (-0.5)


def masked_scores(tile, queries, keys_ref, column_ref, row_ref):
    reach = (tile + 1) * TILE
    scores = dot(keys_ref[0, :reach, :], queries, NT) * SCALING
    same = column_ref[0, :reach, :] == row_ref[0, :, tile * TILE : reach]
    if tile:
        early = jnp.where(same[: tile * TILE], scores[: tile * TILE], MASKED_SCORE)
    own = same[tile * TILE :] & (
        lax.broadcasted_iota(jnp.int32, (TILE, TILE), 0)
        <= lax.broadcasted_iota(jnp.int32, (TILE, TILE), 1)
    )
    own = jnp.where(own, scores[tile * TILE :], MASKED_SCORE)
    return jnp.concatenate([early, own], axis=0) if tile else own


def attention_forward_kernel(
    queries_ref, keys_ref, values_ref, persist_ref, column_ref, row_ref, gate_ref, recalled_ref,
    combined_ref, log_ref,
):
    values_t = values_ref[0].T
    fixed_keys = persist_ref[:PERSIST, :]
    fixed_values_t = persist_ref[PERSIST:, :].astype(F32).T.astype(BF16)
    for tile in range(SEQ_LEN // TILE):
        rows = slice(tile * TILE, (tile + 1) * TILE)
        reach = (tile + 1) * TILE
        queries = queries_ref[0, rows, :]
        scores = masked_scores(tile, queries, keys_ref, column_ref, row_ref)
        fixed = dot(fixed_keys, queries, NT) * SCALING
        highest = jnp.maximum(
            jnp.max(scores, axis=0, keepdims=True), jnp.max(fixed, axis=0, keepdims=True)
        )
        weights = jnp.exp(scores - highest)
        fixed_weights = jnp.exp(fixed - highest)
        totals = jnp.sum(weights, axis=0, keepdims=True) + jnp.sum(
            fixed_weights, axis=0, keepdims=True
        )
        part = 1.0 / totals
        attended = dot(values_t[:, :reach], (weights * part).astype(BF16)) + dot(
            fixed_values_t, (fixed_weights * part).astype(BF16)
        )
        log_ref[0, 0, :, rows] = highest + jnp.log(totals)
        combined_ref[0, rows, :] = (
            attended.T + sigmoid(gate_ref[0, rows, :]) * recalled_ref[0, rows, :]
        ).astype(BF16)


def attention_forward(queries, key_rows, value_rows, persist, documents, gate_pre, recalled):
    rows, width = queries.shape
    sequences, heads = rows // SEQ_LEN, width // HEAD

    def by_seq(values):
        return values.reshape(sequences, SEQ_LEN, width)

    block = pl.BlockSpec((1, SEQ_LEN, HEAD), lambda h, s: (s, 0, h))
    combined, logs = pl.pallas_call(
        attention_forward_kernel,
        grid=(heads, sequences),
        in_specs=[
            block, block, block,
            pl.BlockSpec((2 * PERSIST, HEAD), lambda h, s: (0, h)),
            pl.BlockSpec((1, SEQ_LEN, 1), lambda h, s: (s, 0, 0)),
            pl.BlockSpec((1, 1, SEQ_LEN), lambda h, s: (s, 0, 0)),
            block, block,
        ],
        out_specs=[block, pl.BlockSpec((1, 1, 1, SEQ_LEN), lambda h, s: (s, h, 0, 0))],
        out_shape=[
            jax.ShapeDtypeStruct((sequences, SEQ_LEN, width), BF16),
            jax.ShapeDtypeStruct((sequences, heads, 1, SEQ_LEN), F32),
        ],
        name="attention_forward",
    )(
        by_seq(queries), by_seq(key_rows), by_seq(value_rows), persist,
        documents.reshape(sequences, SEQ_LEN, 1), documents.reshape(sequences, 1, SEQ_LEN),
        by_seq(gate_pre), by_seq(recalled),
    )
    return combined.reshape(rows, width), logs


def attention_backward_kernel(
    queries_ref, keys_ref, values_ref, persist_ref, column_ref, row_ref, log_ref, grad_ref,
    query_mem_ref, key_mem_ref, value_mem_ref,
    query_out, key_out, value_out, persist_out, key_total, value_total,
):
    keys_t = keys_ref[0].T
    fixed_keys = persist_ref[:PERSIST, :]
    fixed_values = persist_ref[PERSIST:, :]
    fixed_keys_t = fixed_keys.astype(F32).T.astype(BF16)

    @pl.when(pl.program_id(1) == 0)
    def _():
        persist_out[...] = jnp.zeros(persist_out.shape, F32)

    for tile in reversed(range(SEQ_LEN // TILE)):
        rows = slice(tile * TILE, (tile + 1) * TILE)
        reach = (tile + 1) * TILE
        queries = queries_ref[0, rows, :]
        grads = grad_ref[0, rows, :]
        logs = log_ref[0, 0, :, rows]
        scores = masked_scores(tile, queries, keys_ref, column_ref, row_ref)
        prob = jnp.exp(scores - logs)
        fixed_prob = jnp.exp(dot(fixed_keys, queries, NT) * SCALING - logs)
        prob_grad = dot(values_ref[0, :reach, :], grads, NT)
        fixed_prob_grad = dot(fixed_values, grads, NT)
        inner = jnp.sum(prob * prob_grad, axis=0, keepdims=True) + jnp.sum(
            fixed_prob * fixed_prob_grad, axis=0, keepdims=True
        )
        score_grad = (prob * (prob_grad - inner)).astype(BF16)
        fixed_score_grad = (fixed_prob * (fixed_prob_grad - inner)).astype(BF16)
        key_part = dot(score_grad, queries)
        value_part = dot(prob.astype(BF16), grads)
        if tile == SEQ_LEN // TILE - 1:
            key_total[...] = key_part
            value_total[...] = value_part
        else:
            key_total[:reach, :] += key_part
            value_total[:reach, :] += value_part
        persist_out[:PERSIST, :] += SCALING * dot(fixed_score_grad, queries)
        persist_out[PERSIST:, :] += dot(fixed_prob.astype(BF16), grads)
        query_part = dot(keys_t[:, :reach], score_grad) + dot(fixed_keys_t, fixed_score_grad)
        query_out[0, rows, :] = (SCALING * query_part.T + query_mem_ref[0, rows, :]).astype(BF16)
    key_out[0] = (SCALING * key_total[...] + key_mem_ref[0]).astype(BF16)
    value_out[0] = (value_total[...] + value_mem_ref[0]).astype(BF16)


def attention_backward(
    queries, key_rows, value_rows, persist, documents, logs, attended_grad,
    query_mem, key_mem, value_mem,
):
    rows, width = queries.shape
    sequences, heads = rows // SEQ_LEN, width // HEAD

    def by_seq(values):
        return values.reshape(sequences, SEQ_LEN, width)

    block = pl.BlockSpec((1, SEQ_LEN, HEAD), lambda h, s: (s, 0, h))
    fixed = pl.BlockSpec((2 * PERSIST, HEAD), lambda h, s: (0, h))
    shape = jax.ShapeDtypeStruct((sequences, SEQ_LEN, width), BF16)
    query_back, key_back, value_back, persist_grad = pl.pallas_call(
        attention_backward_kernel,
        grid=(heads, sequences),
        in_specs=[
            block, block, block, fixed,
            pl.BlockSpec((1, SEQ_LEN, 1), lambda h, s: (s, 0, 0)),
            pl.BlockSpec((1, 1, SEQ_LEN), lambda h, s: (s, 0, 0)),
            pl.BlockSpec((1, 1, 1, SEQ_LEN), lambda h, s: (s, h, 0, 0)),
            block, block, block, block,
        ],
        out_specs=[block, block, block, fixed],
        out_shape=[shape, shape, shape, jax.ShapeDtypeStruct((2 * PERSIST, width), F32)],
        scratch_shapes=[pltpu.VMEM((SEQ_LEN, HEAD), F32)] * 2,
        name="attention_backward",
    )(
        by_seq(queries), by_seq(key_rows), by_seq(value_rows), persist,
        documents.reshape(sequences, SEQ_LEN, 1), documents.reshape(sequences, 1, SEQ_LEN),
        logs, by_seq(attended_grad), by_seq(query_mem), by_seq(key_mem), by_seq(value_mem),
    )
    return tuple(x.reshape(rows, width) for x in (query_back, key_back, value_back)) + (persist_grad,)


EPSILON = 1e-05


def turn(left, right):
    return lax.dot_general(left, right, TN, preferred_element_type=F32)


def matmul(left, right):
    return lax.dot_general(left, right, NN, preferred_element_type=F32)


def matmul_right(left, right):
    return lax.dot_general(left, right, NT, preferred_element_type=F32)


def rms_norm(values, gain):
    return values * lax.rsqrt(jnp.mean(values * values, axis=-1, keepdims=True) + EPSILON) * gain


def norm_back(values, gain, grads):
    scale = lax.rsqrt(jnp.mean(values * values, axis=-1, keepdims=True) + EPSILON)
    weighted = grads * gain
    inner = jnp.mean(values * weighted, axis=-1, keepdims=True)
    return scale * weighted - values * (scale * scale * scale * inner), jnp.sum(
        grads * values * scale, axis=0
    )


class Group:
    def __init__(self):
        self.size = lax.axis_size("tp")
        self.rank = lax.axis_index("tp")

    def swap(self, values):
        return lax.ppermute(values, "tp", [(0, 1), (1, 0)])

    def spread(self, own):
        if self.size == 2:
            return [own, self.swap(own)]
        return [lax.all_gather(own, "tp", axis=0, tiled=True)]

    def collect(self, chunks):
        if self.size == 2:
            other = self.swap(chunks[1].astype(BF16))
            return chunks[0] + other.astype(F32)
        return lax.psum_scatter(
            chunks[0].astype(BF16), "tp", scatter_dimension=0, tiled=True
        ).astype(F32)

    def ordered(self, chunks):
        if self.size == 2:
            own, other = chunks
            first = self.rank == 0
            return jnp.concatenate(
                [jnp.where(first, own, other), jnp.where(first, other, own)], axis=0
            )
        return chunks[0]

    def chunks(self, rows):
        if self.size == 2:
            half = rows.shape[0] // 2
            return [
                lax.dynamic_slice_in_dim(rows, self.rank * half, half),
                lax.dynamic_slice_in_dim(rows, (1 - self.rank) * half, half),
            ]
        return [rows]


def gather_packed(parts):
    local = parts[0].shape[0]
    flat = [part.reshape(local, -1) for part in parts]
    widths = [part.shape[1] for part in flat]
    spare = -sum(widths) % 128
    if spare:
        flat.append(jnp.zeros((local, spare), flat[0].dtype))
    whole = lax.all_gather(jnp.concatenate(flat, axis=1), "fsdp", axis=0, tiled=True)
    outs, at = [], 0
    for width in widths:
        outs.append(whole[:, at : at + width])
        at += width
    return outs


def scatter_packed(parts, local):
    widths = [part.shape[1] for part in parts]
    flat = [part.astype(BF16) for part in parts]
    spare = -sum(widths) % 128
    if spare:
        flat.append(jnp.zeros((flat[0].shape[0], spare), BF16))
    total = lax.psum_scatter(
        jnp.concatenate(flat, axis=1), "fsdp", scatter_dimension=0, tiled=True
    ).astype(F32)
    outs, at = [], 0
    for width in widths:
        outs.append(total[:, at : at + width])
        at += width
    return outs


def on_device(
    tokens,
    norm_gains,
    query_weight,
    key_weight,
    value_weight,
    mix_gate_weight,
    output_weight,
    persistent_tokens,
    memory_init,
    gate_weight,
    up_weight,
    down_weight,
    doc_ids,
    span_starts,
    memory_rates,
    out_grad,
):
    group = Group()
    fsdp = lax.axis_size("fsdp")
    local = query_weight.shape[0]
    width = query_weight.shape[1]
    shares = fsdp * local
    token_chunks = group.spread(tokens)
    grad_chunks = group.spread(out_grad)
    w_query, w_key, w_value, w_mix, packed_init, packed_persist, packed_gains = gather_packed(
        [
            query_weight,
            key_weight,
            value_weight,
            mix_gate_weight,
            memory_init.T.reshape(local, -1),
            persistent_tokens.reshape(local, -1),
            norm_gains.T,
        ]
    )
    w_out, w_gate, w_up, w_down = gather_packed(
        [output_weight.T, gate_weight, up_weight, down_weight.T]
    )
    init = packed_init.reshape(2 * HEAD, width).T.astype(F32)
    persist = packed_persist.reshape(2 * PERSIST, width)
    gains = packed_gains.T.astype(F32)

    rows_in = tokens.astype(F32)
    normed_all = group.ordered(
        [rms_norm(chunk.astype(F32), gains[0]).astype(BF16) for chunk in token_chunks]
    )
    queries = matmul(normed_all, w_query).astype(BF16)
    key_rows = matmul(normed_all, w_key).astype(BF16)
    value_rows = matmul(normed_all, w_value).astype(BF16)
    gate_pre = matmul(normed_all, w_mix)
    doc_blocks = doc_ids.reshape(-1, SPAN)
    live = (doc_blocks == doc_blocks[:, SPAN - 1 :]).astype(F32) / SPAN
    recalled, states = memory_forward(
        queries, key_rows, value_rows, live, span_starts, memory_rates, init
    )
    combined, logs = attention_forward(
        queries, key_rows, value_rows, persist, doc_ids, gate_pre, recalled
    )
    branch = group.collect([matmul_right(chunk, w_out) for chunk in group.chunks(combined)])
    hidden_one = rows_in + branch
    normed_two = rms_norm(hidden_one, gains[1]).astype(BF16)
    normed_chunks = group.spread(normed_two)

    ffn, back_chunks, gate_backs, up_backs, hiddens = [], [], [], [], []
    for rows, grads in zip(normed_chunks, grad_chunks):
        gate_rows = matmul(rows, w_gate)
        up_rows = matmul(rows, w_up)
        gate_sigmoid = jax.nn.sigmoid(gate_rows)
        hidden = (gate_rows * gate_sigmoid * up_rows).astype(BF16)
        hidden_grad = matmul(grads, w_down)
        gate_back = (
            hidden_grad * up_rows * gate_sigmoid * (1.0 + gate_rows * (1.0 - gate_sigmoid))
        ).astype(BF16)
        up_back = (hidden_grad * gate_rows * gate_sigmoid).astype(BF16)
        ffn.append(matmul_right(hidden, w_down))
        back_chunks.append(matmul_right(gate_back, w_gate) + matmul_right(up_back, w_up))
        hiddens.append(hidden)
        gate_backs.append(gate_back)
        up_backs.append(up_back)
    output = (hidden_one + group.collect(ffn)).astype(BF16)
    normed_two_grad = group.collect(back_chunks)
    inner_grad, gain_two_grad = norm_back(hidden_one, gains[1], normed_two_grad)
    hidden_one_grad = out_grad.astype(F32) + inner_grad
    branch_rows = group.ordered(group.spread(hidden_one_grad.astype(BF16)))

    normed_two_all = jnp.concatenate(normed_chunks, axis=0)
    hidden_all = jnp.concatenate(hiddens, axis=0)
    down_grad = turn(jnp.concatenate(grad_chunks, axis=0), hidden_all)
    gate_grad = turn(normed_two_all, jnp.concatenate(gate_backs, axis=0))
    up_grad = turn(normed_two_all, jnp.concatenate(up_backs, axis=0))
    out_weight_grad = turn(branch_rows, combined)
    combined_grad = matmul(branch_rows, w_out)
    out_weight_out, gate_out, up_out, down_out = scatter_packed(
        [out_weight_grad, gate_grad, up_grad, down_grad], local
    )

    attended_grad = combined_grad.astype(BF16)
    gate_open = jax.nn.sigmoid(gate_pre)
    gate_pre_grad = (combined_grad * recalled * gate_open * (1.0 - gate_open)).astype(BF16)
    recalled_grad = combined_grad * gate_open
    query_mem, key_mem, value_mem, init_grad = memory_backward(
        queries, key_rows, value_rows, live, span_starts, memory_rates, recalled_grad, states
    )
    query_back, key_back, value_back, persist_grad = attention_backward(
        queries, key_rows, value_rows, persist, doc_ids, logs, attended_grad,
        query_mem, key_mem, value_mem,
    )
    backs = [query_back, key_back, value_back, gate_pre_grad]
    weights = [w_query, w_key, w_value, w_mix]
    pieces = [group.chunks(back) for back in backs]
    normed_grad = group.collect(
        [
            sum(matmul_right(piece[i], weight) for piece, weight in zip(pieces, weights))
            for i in range(len(pieces[0]))
        ]
    )
    query_out, key_out, value_out, mix_out, init_out, persist_out = scatter_packed(
        [turn(normed_all, back) for back in backs]
        + [init_grad.T.reshape(shares, -1), persist_grad.reshape(shares, -1)],
        local,
    )
    input_grad, gain_one_grad = norm_back(rows_in, gains[0], normed_grad)
    tokens_grad = (hidden_one_grad + input_grad).astype(BF16)
    gain_terms = jnp.stack([gain_one_grad, gain_two_grad]).reshape(2, fsdp, local)
    gain_terms = lax.all_to_all(gain_terms.transpose(1, 0, 2), "fsdp", 0, 0, tiled=True)
    gains_grad = lax.psum(jnp.sum(gain_terms, axis=0), "tp")
    return (
        output,
        tokens_grad,
        gains_grad,
        query_out,
        key_out,
        value_out,
        mix_out,
        out_weight_out.T,
        persist_out.reshape(persistent_tokens.shape),
        init_out.reshape(-1, width).T,
        gate_out,
        up_out,
        down_out.T,
    )


def solution(mesh):
    placed = (
        P(("fsdp", "tp"), None),
        P(None, "fsdp"),
        P("fsdp", "tp"),
        P("fsdp", "tp"),
        P("fsdp", "tp"),
        P("fsdp", "tp"),
        P("tp", "fsdp"),
        P("fsdp", "tp"),
        P("tp", "fsdp"),
        P("fsdp", "tp"),
        P("fsdp", "tp"),
        P("tp", "fsdp"),
        P("fsdp"),
        P("fsdp"),
        P(None, "fsdp", "tp"),
        P(("fsdp", "tp"), None),
    )
    return jax.shard_map(
        on_device,
        mesh=mesh,
        in_specs=placed,
        out_specs=(
            P(("fsdp", "tp"), None),
            P(("fsdp", "tp"), None),
            P(None, "fsdp"),
            P("fsdp", "tp"),
            P("fsdp", "tp"),
            P("fsdp", "tp"),
            P("fsdp", "tp"),
            P("tp", "fsdp"),
            P("fsdp", "tp"),
            P("tp", "fsdp"),
            P("fsdp", "tp"),
            P("fsdp", "tp"),
            P("tp", "fsdp"),
        ),
        check_vma=False,
    )
```

```python
import functools
import jax, jax.numpy as jnp
from jax import lax
from jax.experimental import pallas as pl
from jax.experimental.pallas import tpu as pltpu
from jax.sharding import PartitionSpec as P

HEAD = 128
SPAN = 64
SEQ_LEN = 1024
BF16 = jnp.bfloat16
F32 = jnp.float32
NN = (((1,), (0,)), ((), ()))
NT = (((1,), (1,)), ((), ()))
TN = (((0,), (0,)), ((), ()))


def dot(left, right, dims=NN):
    return lax.dot_general(left, right, dims, preferred_element_type=F32)


def sigmoid(values):
    return 0.5 * jnp.tanh(0.5 * values) + 0.5


def cost(microseconds, nbytes):
    return pl.CostEstimate(
        flops=int(microseconds * 1e9), bytes_accessed=int(nbytes), transcendentals=0
    )


def memory_forward_kernel(
    unroll, sequences, heads, starts_ref, rates_ref, queries_ref, keys_ref, values_ref, live_ref,
    init_ref, recalled_ref, states_ref, first_ref, second_ref, moment_one_ref, moment_two_ref,
):
    spans = SEQ_LEN // SPAN
    step = pl.program_id(0)
    chains = [(s, h) for s in range(sequences) for h in range(heads)]

    @pl.when(step == 0)
    def _():
        for place, (s, h) in enumerate(chains):
            first_ref[place] = jnp.zeros((HEAD, HEAD), F32)
            second_ref[place] = jnp.zeros((HEAD, HEAD), F32)
            moment_one_ref[place] = jnp.zeros((HEAD, HEAD), F32)
            moment_two_ref[place] = jnp.zeros((HEAD, HEAD), F32)

    state = [
        (first_ref[i], second_ref[i], moment_one_ref[i], moment_two_ref[i])
        for i in range(len(chains))
    ]
    for part in range(unroll):
        rows = pl.ds(part * SPAN, SPAN)
        span = step * unroll + part
        begins = [starts_ref[s * spans + span] != 0 for s in range(sequences)]
        used = []
        for place, (s, h) in enumerate(chains):
            one, two, moment_one, moment_two = state[place]
            start = init_ref[pl.ds(h * HEAD, HEAD), :]
            used.append(
                (
                    jnp.where(begins[s], start[:, :HEAD], one),
                    jnp.where(begins[s], start[:, HEAD:], two),
                    jnp.where(begins[s], 0.0, moment_one),
                    jnp.where(begins[s], 0.0, moment_two),
                )
            )
        low = [(one.astype(BF16), two.astype(BF16)) for one, two, _, _ in used]
        for place in range(len(chains)):
            states_ref[part, place, :, :HEAD] = low[place][0]
            states_ref[part, place, :, HEAD:] = low[place][1]
        cols = [pl.ds(h * HEAD, HEAD) for _, h in chains]
        keys = [keys_ref[s, rows, cols[i]] for i, (s, _) in enumerate(chains)]
        hidden = [dot(keys[i], low[i][0]) for i in range(len(chains))]
        gates = [sigmoid(value) for value in hidden]
        active = [(h * g).astype(BF16) for h, g in zip(hidden, gates)]
        outs = [dot(active[i], low[i][1]) for i in range(len(chains))]
        errors = [
            ((outs[i] - values_ref[s, rows, cols[i]].astype(F32)) * live_ref[s, rows, :]).astype(BF16)
            for i, (s, _) in enumerate(chains)
        ]
        back = [dot(errors[i], low[i][1], NT) for i in range(len(chains))]
        inner = [
            (b * (g * (1.0 + h * (1.0 - g)))).astype(BF16)
            for b, h, g in zip(back, hidden, gates)
        ]
        grad_one = [dot(keys[i], inner[i], TN) for i in range(len(chains))]
        grad_two = [dot(active[i], errors[i], TN) for i in range(len(chains))]
        state = []
        for place, (s, h) in enumerate(chains):
            one, two, moment_one, moment_two = used[place]
            index = (s * spans + span) * heads + h
            stride = sequences * spans * heads
            momentum = rates_ref[index]
            size = rates_ref[stride + index]
            keep = 1.0 - rates_ref[2 * stride + index]
            moment_one = momentum * moment_one - size * grad_one[place]
            moment_two = momentum * moment_two - size * grad_two[place]
            state.append((keep * one + moment_one, keep * two + moment_two, moment_one, moment_two))
        for place, (s, h) in enumerate(chains):
            asked = dot(queries_ref[s, rows, cols[place]], low[place][0])
            asked = (asked * sigmoid(asked)).astype(BF16)
            recalled_ref[s, rows, cols[place]] = dot(asked, low[place][1]).astype(recalled_ref.dtype)
    for place in range(len(chains)):
        first_ref[place], second_ref[place], moment_one_ref[place], moment_two_ref[place] = state[place]


def memory_forward(queries, key_rows, value_rows, live, starts, rates, init, unroll=2):
    rows, width = queries.shape
    sequences, heads = rows // SEQ_LEN, width // HEAD
    spans = SEQ_LEN // SPAN
    chains = sequences * heads

    def by_seq(values):
        return values.reshape(sequences, SEQ_LEN, width)

    block = pl.BlockSpec((sequences, unroll * SPAN, width), lambda c: (0, c, 0))
    smem = pl.BlockSpec(memory_space=pltpu.SMEM)
    recalled, states = pl.pallas_call(
        functools.partial(memory_forward_kernel, unroll, sequences, heads),
        grid=(spans // unroll,),
        in_specs=[
            smem, smem, block, block, block,
            pl.BlockSpec((sequences, unroll * SPAN, 1), lambda c: (0, c, 0)),
            pl.BlockSpec((heads * HEAD, 2 * HEAD), lambda c: (0, 0)),
        ],
        out_specs=[
            block,
            pl.BlockSpec((unroll, chains, HEAD, 2 * HEAD), lambda c: (c, 0, 0, 0)),
        ],
        out_shape=[
            jax.ShapeDtypeStruct((sequences, SEQ_LEN, width), F32),
            jax.ShapeDtypeStruct((spans, chains, HEAD, 2 * HEAD), BF16),
        ],
        scratch_shapes=[pltpu.VMEM((chains, HEAD, HEAD), F32)] * 4,
        cost_estimate=cost(14, 0),
        name="memory_forward",
    )(
        starts, rates.reshape(-1), by_seq(queries), by_seq(key_rows), by_seq(value_rows),
        live.reshape(sequences, SEQ_LEN, 1), init,
    )
    return recalled.reshape(rows, width), states


def memory_backward_kernel(
    unroll, sequences, heads, starts_ref, rates_ref, queries_ref, keys_ref, values_ref, live_ref,
    grads_ref, states_ref, query_out, key_out, value_out, init_out,
    first_ref, second_ref, moment_one_ref, moment_two_ref, total_ref,
):
    spans = SEQ_LEN // SPAN
    step = pl.program_id(0)
    chains = [(s, h) for s in range(sequences) for h in range(heads)]
    count = len(chains)
    zero = jnp.zeros((HEAD, HEAD), F32)

    @pl.when(step == 0)
    def _():
        for i in range(count):
            first_ref[i] = zero
            second_ref[i] = zero
            moment_one_ref[i] = zero
            moment_two_ref[i] = zero
            total_ref[i] = jnp.zeros((HEAD, 2 * HEAD), F32)

    state = [(first_ref[i], second_ref[i], moment_one_ref[i], moment_two_ref[i]) for i in range(count)]
    cols = [pl.ds(h * HEAD, HEAD) for _, h in chains]
    for part in reversed(range(unroll)):
        rows = pl.ds(part * SPAN, SPAN)
        span = spans - (step + 1) * unroll + part
        stride = sequences * spans * heads
        each = range(count)
        one = [states_ref[part, i, :, :HEAD] for i in each]
        two = [states_ref[part, i, :, HEAD:] for i in each]
        queries = [queries_ref[chains[i][0], rows, cols[i]] for i in each]
        keys = [keys_ref[chains[i][0], rows, cols[i]] for i in each]
        values = [values_ref[chains[i][0], rows, cols[i]].astype(F32) for i in each]
        live = [live_ref[chains[i][0], rows, :] for i in each]
        grads = [grads_ref[chains[i][0], rows, cols[i]].astype(BF16) for i in each]
        hidden = [dot(keys[i], one[i]) for i in each]
        gates = [sigmoid(hidden[i]) for i in each]
        active = [(hidden[i] * gates[i]).astype(BF16) for i in each]
        errors = [((dot(active[i], two[i]) - values[i]) * live[i]).astype(BF16) for i in each]
        back = [dot(errors[i], two[i], NT) for i in each]
        slope = [gates[i] * (1.0 + hidden[i] * (1.0 - gates[i])) for i in each]
        bend = [
            gates[i] * (1.0 - gates[i]) * (2.0 + hidden[i] * (1.0 - 2.0 * gates[i])) * back[i]
            for i in each
        ]
        inner = [(back[i] * slope[i]).astype(BF16) for i in each]
        asked = [dot(queries[i], one[i]) for i in each]
        asked_gate = [sigmoid(asked[i]) for i in each]
        asked_active = [(asked[i] * asked_gate[i]).astype(BF16) for i in each]
        asked_grad = [
            (
                dot(grads[i], two[i], NT)
                * (asked_gate[i] * (1.0 + asked[i] * (1.0 - asked_gate[i])))
            ).astype(BF16)
            for i in each
        ]
        for i in each:
            query_out[chains[i][0], rows, cols[i]] = dot(asked_grad[i], one[i], NT)
        momentum, size, keep = [], [], []
        for s, h in chains:
            index = (s * spans + span) * heads + h
            momentum.append(rates_ref[index])
            size.append(rates_ref[stride + index])
            keep.append(1.0 - rates_ref[2 * stride + index])
        sum_one = [state[i][0] + state[i][2] for i in each]
        sum_two = [state[i][1] + state[i][3] for i in each]
        step_one = [(-size[i] * sum_one[i]).astype(BF16) for i in each]
        step_two = [(-size[i] * sum_two[i]).astype(BF16) for i in each]
        inner_grad = [dot(keys[i], step_one[i]) for i in each]
        back_grad = [(inner_grad[i] * slope[i]).astype(BF16) for i in each]
        error_grad = [
            (dot(back_grad[i], two[i]) + dot(active[i], step_two[i])) * live[i] for i in each
        ]
        for i in each:
            value_out[chains[i][0], rows, cols[i]] = -error_grad[i]
        out_grad = [error_grad[i].astype(BF16) for i in each]
        active_grad = [dot(errors[i], step_two[i], NT) + dot(out_grad[i], two[i], NT) for i in each]
        hidden_grad = [
            (active_grad[i] * slope[i] + inner_grad[i] * bend[i]).astype(BF16) for i in each
        ]
        new_one = [
            keep[i] * state[i][0] + dot(keys[i], hidden_grad[i], TN) + dot(queries[i], asked_grad[i], TN)
            for i in each
        ]
        new_two = [
            keep[i] * state[i][1]
            + dot(back_grad[i], errors[i], TN)
            + dot(active[i], out_grad[i], TN)
            + dot(asked_active[i], grads[i], TN)
            for i in each
        ]
        for i in each:
            key_out[chains[i][0], rows, cols[i]] = dot(inner[i], step_one[i], NT) + dot(
                hidden_grad[i], one[i], NT
            )
        begins = [starts_ref[s * spans + span] != 0 for s in range(sequences)]
        state = []
        for i, (s, h) in enumerate(chains):
            begin = begins[s]
            total_ref[i, :, :HEAD] += jnp.where(begin, new_one[i], 0.0)
            total_ref[i, :, HEAD:] += jnp.where(begin, new_two[i], 0.0)
            state.append(
                (
                    jnp.where(begin, 0.0, new_one[i]),
                    jnp.where(begin, 0.0, new_two[i]),
                    jnp.where(begin, 0.0, momentum[i] * sum_one[i]),
                    jnp.where(begin, 0.0, momentum[i] * sum_two[i]),
                )
            )
    for i in range(count):
        first_ref[i], second_ref[i], moment_one_ref[i], moment_two_ref[i] = state[i]

    @pl.when(step == pl.num_programs(0) - 1)
    def _():
        for h in range(heads):
            init_out[pl.ds(h * HEAD, HEAD), :] = sum(
                total_ref[s * heads + h] for s in range(sequences)
            )


def memory_backward(
    queries, key_rows, value_rows, live, starts, rates, grads, states, unroll=2
):
    rows, width = queries.shape
    sequences, heads = rows // SEQ_LEN, width // HEAD
    spans = SEQ_LEN // SPAN
    chains = sequences * heads
    steps = spans // unroll

    def by_seq(values):
        return values.reshape(sequences, SEQ_LEN, width)

    block = pl.BlockSpec((sequences, unroll * SPAN, width), lambda c: (0, steps - 1 - c, 0))
    smem = pl.BlockSpec(memory_space=pltpu.SMEM)
    shape = jax.ShapeDtypeStruct((sequences, SEQ_LEN, width), F32)
    query_mem, key_mem, value_mem, init_grad = pl.pallas_call(
        functools.partial(memory_backward_kernel, unroll, sequences, heads),
        grid=(steps,),
        in_specs=[
            smem, smem, block, block, block,
            pl.BlockSpec((sequences, unroll * SPAN, 1), lambda c: (0, steps - 1 - c, 0)),
            block,
            pl.BlockSpec((unroll, chains, HEAD, 2 * HEAD), lambda c: (steps - 1 - c, 0, 0, 0)),
        ],
        out_specs=[
            block, block, block,
            pl.BlockSpec((heads * HEAD, 2 * HEAD), lambda c: (0, 0)),
        ],
        out_shape=[
            shape, shape, shape,
            jax.ShapeDtypeStruct((heads * HEAD, 2 * HEAD), F32),
        ],
        scratch_shapes=[pltpu.VMEM((chains, HEAD, HEAD), F32)] * 4
        + [pltpu.VMEM((chains, HEAD, 2 * HEAD), F32)],
        cost_estimate=cost(27, 0),
        name="memory_backward",
    )(
        starts, rates.reshape(-1), by_seq(queries), by_seq(key_rows), by_seq(value_rows),
        live.reshape(sequences, SEQ_LEN, 1), by_seq(grads), states,
    )
    return tuple(x.reshape(rows, width) for x in (query_mem, key_mem, value_mem)) + (init_grad,)

PERSIST = 16
TILE = 256
MASKED_SCORE = -1e30
SCALING = HEAD ** (-0.5)


def masked_scores(tile, queries, keys_ref, column_ref, row_ref):
    reach = (tile + 1) * TILE
    scores = dot(keys_ref[0, :reach, :], queries, NT) * SCALING
    same = column_ref[0, :reach, :] == row_ref[0, :, tile * TILE : reach]
    if tile:
        early = jnp.where(same[: tile * TILE], scores[: tile * TILE], MASKED_SCORE)
    own = same[tile * TILE :] & (
        lax.broadcasted_iota(jnp.int32, (TILE, TILE), 0)
        <= lax.broadcasted_iota(jnp.int32, (TILE, TILE), 1)
    )
    own = jnp.where(own, scores[tile * TILE :], MASKED_SCORE)
    return jnp.concatenate([early, own], axis=0) if tile else own


def attention_forward_kernel(
    queries_ref, keys_ref, values_ref, persist_ref, column_ref, row_ref, gate_ref, recalled_ref,
    after_ref, combined_ref, log_ref,
):
    values_t = values_ref[0].T
    fixed_keys = persist_ref[:PERSIST, :]
    fixed_values_t = persist_ref[PERSIST:, :].astype(F32).T.astype(BF16)
    for tile in range(SEQ_LEN // TILE):
        rows = slice(tile * TILE, (tile + 1) * TILE)
        reach = (tile + 1) * TILE
        queries = queries_ref[0, rows, :]
        scores = masked_scores(tile, queries, keys_ref, column_ref, row_ref)
        fixed = dot(fixed_keys, queries, NT) * SCALING
        highest = jnp.maximum(
            jnp.max(scores, axis=0, keepdims=True), jnp.max(fixed, axis=0, keepdims=True)
        )
        weights = jnp.exp(scores - highest)
        fixed_weights = jnp.exp(fixed - highest)
        totals = jnp.sum(weights, axis=0, keepdims=True) + jnp.sum(
            fixed_weights, axis=0, keepdims=True
        )
        part = 1.0 / totals
        attended = dot(values_t[:, :reach], (weights * part).astype(BF16)) + dot(
            fixed_values_t, (fixed_weights * part).astype(BF16)
        )
        log_ref[0, 0, :, rows] = highest + jnp.log(totals)
        combined_ref[0, rows, :] = (
            attended.T + sigmoid(gate_ref[0, rows, :]) * recalled_ref[0, rows, :]
        ).astype(BF16)


def attention_forward(
    queries, key_rows, value_rows, persist, documents, gate_pre, recalled, after
):
    rows, width = queries.shape
    sequences, heads = rows // SEQ_LEN, width // HEAD

    def by_seq(values):
        return values.reshape(sequences, SEQ_LEN, width)

    block = pl.BlockSpec((1, SEQ_LEN, HEAD), lambda h, s: (s, 0, h))
    combined, logs = pl.pallas_call(
        attention_forward_kernel,
        grid=(heads, sequences),
        in_specs=[
            block, block, block,
            pl.BlockSpec((2 * PERSIST, HEAD), lambda h, s: (0, h)),
            pl.BlockSpec((1, SEQ_LEN, 1), lambda h, s: (s, 0, 0)),
            pl.BlockSpec((1, 1, SEQ_LEN), lambda h, s: (s, 0, 0)),
            block, block, pl.BlockSpec(memory_space=pl.ANY),
        ],
        out_specs=[block, pl.BlockSpec((1, 1, 1, SEQ_LEN), lambda h, s: (s, h, 0, 0))],
        out_shape=[
            jax.ShapeDtypeStruct((sequences, SEQ_LEN, width), BF16),
            jax.ShapeDtypeStruct((sequences, heads, 1, SEQ_LEN), F32),
        ],
        cost_estimate=cost(12, 0),
        name="attention_forward",
    )(
        by_seq(queries), by_seq(key_rows), by_seq(value_rows), persist,
        documents.reshape(sequences, SEQ_LEN, 1), documents.reshape(sequences, 1, SEQ_LEN),
        by_seq(gate_pre), by_seq(recalled), after,
    )
    return combined.reshape(rows, width), logs


def attention_backward_kernel(
    queries_ref, keys_ref, values_ref, persist_ref, column_ref, row_ref, log_ref, grad_ref,
    query_mem_ref, key_mem_ref, value_mem_ref,
    query_out, key_out, value_out, persist_out, key_total, value_total,
):
    keys_t = keys_ref[0].T
    fixed_keys = persist_ref[:PERSIST, :]
    fixed_values = persist_ref[PERSIST:, :]
    fixed_keys_t = fixed_keys.astype(F32).T.astype(BF16)

    @pl.when(pl.program_id(1) == 0)
    def _():
        persist_out[...] = jnp.zeros(persist_out.shape, F32)

    for tile in reversed(range(SEQ_LEN // TILE)):
        rows = slice(tile * TILE, (tile + 1) * TILE)
        reach = (tile + 1) * TILE
        queries = queries_ref[0, rows, :]
        grads = grad_ref[0, rows, :]
        logs = log_ref[0, 0, :, rows]
        scores = masked_scores(tile, queries, keys_ref, column_ref, row_ref)
        prob = jnp.exp(scores - logs)
        fixed_prob = jnp.exp(dot(fixed_keys, queries, NT) * SCALING - logs)
        prob_grad = dot(values_ref[0, :reach, :], grads, NT)
        fixed_prob_grad = dot(fixed_values, grads, NT)
        inner = jnp.sum(prob * prob_grad, axis=0, keepdims=True) + jnp.sum(
            fixed_prob * fixed_prob_grad, axis=0, keepdims=True
        )
        score_grad = (prob * (prob_grad - inner)).astype(BF16)
        fixed_score_grad = (fixed_prob * (fixed_prob_grad - inner)).astype(BF16)
        key_part = dot(score_grad, queries)
        value_part = dot(prob.astype(BF16), grads)
        if tile == SEQ_LEN // TILE - 1:
            key_total[...] = key_part
            value_total[...] = value_part
        else:
            key_total[:reach, :] += key_part
            value_total[:reach, :] += value_part
        persist_out[:PERSIST, :] += SCALING * dot(fixed_score_grad, queries)
        persist_out[PERSIST:, :] += dot(fixed_prob.astype(BF16), grads)
        query_part = dot(keys_t[:, :reach], score_grad) + dot(fixed_keys_t, fixed_score_grad)
        query_out[0, rows, :] = (SCALING * query_part.T + query_mem_ref[0, rows, :]).astype(BF16)
    key_out[0] = (SCALING * key_total[...] + key_mem_ref[0]).astype(BF16)
    value_out[0] = (value_total[...] + value_mem_ref[0]).astype(BF16)


def attention_backward(
    queries, key_rows, value_rows, persist, documents, logs, attended_grad,
    query_mem, key_mem, value_mem,
):
    rows, width = queries.shape
    sequences, heads = rows // SEQ_LEN, width // HEAD

    def by_seq(values):
        return values.reshape(sequences, SEQ_LEN, width)

    block = pl.BlockSpec((1, SEQ_LEN, HEAD), lambda h, s: (s, 0, h))
    fixed = pl.BlockSpec((2 * PERSIST, HEAD), lambda h, s: (0, h))
    shape = jax.ShapeDtypeStruct((sequences, SEQ_LEN, width), BF16)
    query_back, key_back, value_back, persist_grad = pl.pallas_call(
        attention_backward_kernel,
        grid=(heads, sequences),
        in_specs=[
            block, block, block, fixed,
            pl.BlockSpec((1, SEQ_LEN, 1), lambda h, s: (s, 0, 0)),
            pl.BlockSpec((1, 1, SEQ_LEN), lambda h, s: (s, 0, 0)),
            pl.BlockSpec((1, 1, 1, SEQ_LEN), lambda h, s: (s, h, 0, 0)),
            block, block, block, block,
        ],
        out_specs=[block, block, block, fixed],
        out_shape=[shape, shape, shape, jax.ShapeDtypeStruct((2 * PERSIST, width), F32)],
        scratch_shapes=[pltpu.VMEM((SEQ_LEN, HEAD), F32)] * 2,
        cost_estimate=cost(15, 0),
        name="attention_backward",
    )(
        by_seq(queries), by_seq(key_rows), by_seq(value_rows), persist,
        documents.reshape(sequences, SEQ_LEN, 1), documents.reshape(sequences, 1, SEQ_LEN),
        logs, by_seq(attended_grad), by_seq(query_mem), by_seq(key_mem), by_seq(value_mem),
    )
    return tuple(x.reshape(rows, width) for x in (query_back, key_back, value_back)) + (persist_grad,)


EPSILON = 1e-05


def turn(left, right):
    return lax.dot_general(left, right, TN, preferred_element_type=F32)


def matmul(left, right):
    return lax.dot_general(left, right, NN, preferred_element_type=F32)


def matmul_right(left, right):
    return lax.dot_general(left, right, NT, preferred_element_type=F32)


def rms_norm(values, gain):
    return values * lax.rsqrt(jnp.mean(values * values, axis=-1, keepdims=True) + EPSILON) * gain


def norm_back(values, gain, grads):
    scale = lax.rsqrt(jnp.mean(values * values, axis=-1, keepdims=True) + EPSILON)
    weighted = grads * gain
    inner = jnp.mean(values * weighted, axis=-1, keepdims=True)
    return scale * weighted - values * (scale * scale * scale * inner), jnp.sum(
        grads * values * scale, axis=0
    )


def project_kernel(
    halves, half_tiles, rank_ref, gains_ref, *refs
):
    token_refs = refs[:halves]
    weight_ref, normed_out, query_out, key_out, value_out, gate_out = refs[halves:]
    width = query_out.shape[1]
    rows = token_refs[0][...]
    if halves == 2:
        mine = pl.program_id(0) // half_tiles == rank_ref[0]
        rows = jnp.where(mine, rows, token_refs[1][...])
    rows = rows.astype(F32)
    normed = rms_norm(rows, gains_ref[...]).astype(BF16)
    normed_out[...] = normed
    for place, out in enumerate((query_out, key_out, value_out, gate_out)):
        out[...] = dot(normed, weight_ref[:, place * width : (place + 1) * width]).astype(out.dtype)


def project(rank, gain, chunks, weights, width):
    halves = len(chunks)
    depth = chunks[0].shape[1]
    half_tiles = chunks[0].shape[0] // TILE
    rows = halves * chunks[0].shape[0]

    out = pl.BlockSpec((TILE, width), lambda i, rank_ref: (i, 0))
    shape = jax.ShapeDtypeStruct((rows, width), BF16)
    return pl.pallas_call(
        functools.partial(project_kernel, halves, half_tiles),
        grid_spec=pltpu.PrefetchScalarGridSpec(
            num_scalar_prefetch=1,
            grid=(rows // TILE,),
            in_specs=[pl.BlockSpec((1, depth), lambda i, rank_ref: (0, 0))]
            + [
                pl.BlockSpec((TILE, depth), chunk_map(place, half_tiles, halves))
                for place in range(halves)
            ]
            + [
                pl.BlockSpec(
                    (depth, 4 * width), lambda i, rank_ref: (0, 0), pipeline_mode=pl.Buffered(1)
                )
            ],
            out_specs=[pl.BlockSpec((TILE, depth), lambda i, rank_ref: (i, 0))] + [out] * 4,
        ),
        out_shape=[jax.ShapeDtypeStruct((rows, depth), BF16)]
        + [shape] * 3
        + [jax.ShapeDtypeStruct((rows, width), F32)],
        cost_estimate=cost(8, 0),
        name="project",
    )(rank.reshape(1), gain.reshape(1, -1), *chunks, weights)


def project_back_kernel(base_ref, *refs):
    weight_ref, out_ref = refs[-2:]
    width = refs[0].shape[1]
    total = 0.0
    for place, back in enumerate(refs[:-2]):
        total += dot(back[...], weight_ref[:, place * width : (place + 1) * width], NT)
    out_ref[...] = total.astype(out_ref.dtype)


def project_back(base, rows, backs, weights, dtype):
    width = backs[0].shape[1]
    depth = weights.shape[0]
    return pl.pallas_call(
        project_back_kernel,
        grid_spec=pltpu.PrefetchScalarGridSpec(
            num_scalar_prefetch=1,
            grid=(rows // TILE,),
            in_specs=[pl.BlockSpec((TILE, width), lambda i, base_ref: (base_ref[0] + i, 0))] * 4
            + [
                pl.BlockSpec(
                    (depth, 4 * width), lambda i, base_ref: (0, 0), pipeline_mode=pl.Buffered(1)
                )
            ],
            out_specs=pl.BlockSpec((TILE, depth), lambda i, base_ref: (i, 0)),
        ),
        out_shape=jax.ShapeDtypeStruct((rows, depth), dtype),
        cost_estimate=cost(4, 0),
        name="project_back",
    )(jnp.reshape(base, (1,)).astype(jnp.int32), *backs, weights)


def weight_grads_kernel(counts, extra, split, core_ref, *refs):
    at = 0
    parts = []
    for chunk_count, right_count in counts:
        lefts = [ref[...] for ref in refs[at : at + chunk_count]]
        at += chunk_count
        for _ in range(right_count):
            parts.append(
                sum(
                    dot(left, right[...], TN)
                    for left, right in zip(lefts, refs[at : at + chunk_count])
                ).astype(BF16)
            )
            at += chunk_count
    if extra:
        parts.append(refs[at][...])
        at += 1
    outs = refs[at:]
    place = 0
    for part in parts:
        cols = slice(place, place + part.shape[1])
        place += part.shape[1]
        if split:
            local = part.shape[0] // 4
            for y in range(2):
                even = part[2 * y * local : (2 * y + 1) * local]
                odd = part[(2 * y + 1) * local : (2 * y + 2) * local]
                first = core_ref[0] == 0
                outs[0][y, :, cols] = jnp.where(first, even, odd)
                outs[1][y, :, cols] = jnp.where(first, odd, even)
        else:
            outs[0][:, cols] = part


def weight_grads(groups, extra=None, core=None):
    depth = groups[0][0][0].shape[1]
    rights = [right for _, group in groups for right in group]
    total = sum(right[0].shape[1] for right in rights) + (0 if extra is None else extra.shape[1])
    operands, specs, counts = [], [], []
    for lefts, group in groups:
        counts.append((len(lefts), len(group)))
        for left in lefts:
            operands.append(left)
            specs.append(pl.BlockSpec((left.shape[0], TILE), lambda d, core_ref: (0, d)))
        for right in group:
            for chunk in right:
                operands.append(chunk)
                specs.append(
                    pl.BlockSpec(
                        chunk.shape, lambda d, core_ref: (0, 0), pipeline_mode=pl.Buffered(1)
                    )
                )
    if extra is not None:
        operands.append(extra)
        specs.append(pl.BlockSpec((TILE, extra.shape[1]), lambda d, core_ref: (d, 0)))
    if core is None:
        out_specs = pl.BlockSpec((TILE, total), lambda d, core_ref: (d, 0))
        out_shape = jax.ShapeDtypeStruct((depth, total), BF16)
    else:
        out_specs = [pl.BlockSpec((2, TILE // 4, total), lambda d, core_ref: (d, 0, 0))] * 2
        out_shape = [jax.ShapeDtypeStruct((depth * 2 // TILE, TILE // 4, total), BF16)] * 2
    return pl.pallas_call(
        functools.partial(weight_grads_kernel, tuple(counts), extra is not None, core is not None),
        grid_spec=pltpu.PrefetchScalarGridSpec(
            num_scalar_prefetch=1,
            grid=(depth // TILE,),
            in_specs=specs,
            out_specs=out_specs,
        ),
        out_shape=out_shape,
        cost_estimate=cost(total * 3e-3, 0),
        name="weight_grads",
    )(jnp.reshape(0 if core is None else core, (1,)).astype(jnp.int32), *operands)


def open_grads_kernel(halves, half_tiles, passed, rank_ref, *refs):
    grads = refs[0][...].astype(F32)
    if halves == 2:
        mine = pl.program_id(0) // half_tiles == rank_ref[0]
        grads = jnp.where(mine, grads, refs[1][...].astype(F32))
    gate_ref, recalled_ref = refs[halves : halves + 2]
    attended_out, gate_out, recalled_out = refs[halves + 2 + passed : halves + 5 + passed]
    opened = sigmoid(gate_ref[...])
    through = grads * opened
    attended_out[...] = grads.astype(BF16)
    recalled_out[...] = through.astype(BF16)
    gate_out[...] = (through * recalled_ref[...] * (1.0 - opened)).astype(BF16)


def chunk_map(place, half_tiles, halves):
    def index(i, rank_ref):
        start = (rank_ref[0] if place == 0 else 1 - rank_ref[0]) * half_tiles
        return jnp.clip(i - start, 0, half_tiles - 1), 0

    return index if halves == 2 else lambda i, rank_ref: (i, 0)


def open_grads(rank, chunks, gate_pre, recalled, passed):
    halves = len(chunks)
    rows, width = gate_pre.shape
    half_tiles = chunks[0].shape[0] // TILE
    block = pl.BlockSpec((TILE, width), lambda i, rank_ref: (i, 0))
    anywhere = pl.BlockSpec(memory_space=pl.ANY)
    shape = jax.ShapeDtypeStruct((rows, width), BF16)
    first = 1 + halves + 2
    return pl.pallas_call(
        functools.partial(open_grads_kernel, halves, half_tiles, len(passed)),
        grid_spec=pltpu.PrefetchScalarGridSpec(
            num_scalar_prefetch=1,
            grid=(rows // TILE,),
            in_specs=[
                pl.BlockSpec((TILE, width), chunk_map(place, half_tiles, halves))
                for place in range(halves)
            ]
            + [block] * 2
            + [anywhere] * len(passed),
            out_specs=[block] * 3 + [anywhere] * len(passed),
        ),
        out_shape=[shape] * 3 + [jax.ShapeDtypeStruct(x.shape, x.dtype) for x in passed],
        input_output_aliases={first + i: 3 + i for i in range(len(passed))},
        cost_estimate=cost(3, 0),
        name="open_grads",
    )(rank.reshape(1), *chunks, gate_pre, recalled, *passed)


class Group:
    def __init__(self):
        self.size = lax.axis_size("tp")
        self.rank = lax.axis_index("tp")

    def swap(self, values):
        return lax.ppermute(values, "tp", [(0, 1), (1, 0)])

    def spread(self, own):
        if self.size == 2:
            return [own, self.swap(own)]
        return [lax.all_gather(own, "tp", axis=0, tiled=True)]

    def collect(self, chunks):
        if self.size == 2:
            other = self.swap(chunks[1].astype(BF16))
            return chunks[0] + other.astype(F32)
        return lax.psum_scatter(
            chunks[0].astype(BF16), "tp", scatter_dimension=0, tiled=True
        ).astype(F32)

    def ordered(self, chunks):
        if self.size == 2:
            own, other = chunks
            first = self.rank == 0
            return jnp.concatenate(
                [jnp.where(first, own, other), jnp.where(first, other, own)], axis=0
            )
        return chunks[0]

    def chunks(self, rows):
        if self.size == 2:
            half = rows.shape[0] // 2
            return [
                lax.dynamic_slice_in_dim(rows, self.rank * half, half),
                lax.dynamic_slice_in_dim(rows, (1 - self.rank) * half, half),
            ]
        return [rows]


def gather_packed(parts):
    local = parts[0].shape[0]
    flat = [part.reshape(local, -1) for part in parts]
    widths = [part.shape[1] for part in flat]
    spare = -sum(widths) % 128
    if spare:
        flat.append(jnp.zeros((local, spare), flat[0].dtype))
    return lax.all_gather(jnp.concatenate(flat, axis=1), "fsdp", axis=0, tiled=True)


def gather_one(values):
    return lax.all_gather(values, "fsdp", axis=0, tiled=True)


def ring_scatter(mine, theirs):
    place = lax.axis_index("fsdp")
    y, z = (place // 2) % 2, place // 4
    got = lax.ppermute(theirs, "fsdp", [(i, i ^ 1) for i in range(16)])

    def part(step, row):
        at = ((z + 3 - step) % 4) * 2 + row
        return lax.dynamic_index_in_dim(mine, at, 0, keepdims=False).astype(
            F32
        ) + lax.dynamic_index_in_dim(got, at, 0, keepdims=False).astype(F32)

    total = None
    for step in range(4):
        other = part(step, 1 - y).astype(BF16)
        keep = part(step, y) + lax.ppermute(
            other, "fsdp", [(i, i ^ 2) for i in range(16)]
        ).astype(F32)
        if total is not None:
            keep = keep + lax.ppermute(
                total.astype(BF16), "fsdp", [(i, (i + 4) % 16) for i in range(16)]
            ).astype(F32)
        total = keep
    return total


def split_columns(values, widths):
    outs, at = [], 0
    for size in widths:
        outs.append(values[:, at : at + size])
        at += size
    return outs


def on_device(
    tokens,
    norm_gains,
    query_weight,
    key_weight,
    value_weight,
    mix_gate_weight,
    output_weight,
    persistent_tokens,
    memory_init,
    gate_weight,
    up_weight,
    down_weight,
    doc_ids,
    span_starts,
    memory_rates,
    out_grad,
):
    group = Group()
    fsdp = lax.axis_size("fsdp")
    local, width = query_weight.shape
    depth = fsdp * local
    special = group.size == 2 and fsdp == 16 and depth == 4 * TILE
    token_chunks = group.spread(tokens)
    grad_chunks = group.spread(out_grad)
    packed = gather_packed(
        [
            query_weight,
            key_weight,
            value_weight,
            mix_gate_weight,
            memory_init.T.reshape(local, -1),
            persistent_tokens.reshape(local, -1),
            norm_gains.T,
        ]
    )
    spots = [
        4 * width,
        4 * width + 2 * HEAD * width // depth,
        4 * width + (2 * HEAD + 2 * PERSIST) * width // depth,
    ]
    w_out, w_gate, w_up, w_down = split_columns(
        gather_packed([output_weight.T, gate_weight, up_weight, down_weight.T]),
        [width] + [gate_weight.shape[1]] * 3,
    )
    init = packed[:, spots[0] : spots[1]].reshape(2 * HEAD, width).T.astype(F32)
    persist = packed[:, spots[1] : spots[2]].reshape(2 * PERSIST, width)
    gains = packed[:, spots[2] : spots[2] + 2].T.astype(F32)

    rows_in = tokens.astype(F32)
    normed_all, queries, key_rows, value_rows, gate_pre = project(
        group.rank, gains[0], token_chunks, packed, width
    )
    doc_blocks = doc_ids.reshape(-1, SPAN)
    live = (doc_blocks == doc_blocks[:, SPAN - 1 :]).astype(F32) / SPAN
    recalled, states = memory_forward(
        queries, key_rows, value_rows, live, span_starts, memory_rates, init
    )
    combined, logs = attention_forward(
        queries, key_rows, value_rows, persist, doc_ids, gate_pre, recalled, grad_chunks[-1]
    )
    branch = group.collect([matmul_right(chunk, w_out) for chunk in group.chunks(combined)])
    hidden_one = rows_in + branch
    normed_two = rms_norm(hidden_one, gains[1]).astype(BF16)
    normed_chunks = group.spread(normed_two)

    ffn, back_chunks, gate_backs, up_backs, hiddens = [], [], [], [], []
    for rows, grads in zip(normed_chunks, grad_chunks):
        gate_rows = matmul(rows, w_gate)
        up_rows = matmul(rows, w_up)
        gate_sigmoid = jax.nn.sigmoid(gate_rows)
        hidden = (gate_rows * gate_sigmoid * up_rows).astype(BF16)
        hidden_grad = matmul(grads, w_down)
        gate_back = (
            hidden_grad * up_rows * gate_sigmoid * (1.0 + gate_rows * (1.0 - gate_sigmoid))
        ).astype(BF16)
        up_back = (hidden_grad * gate_rows * gate_sigmoid).astype(BF16)
        ffn.append(matmul_right(hidden, w_down))
        back_chunks.append(matmul_right(gate_back, w_gate) + matmul_right(up_back, w_up))
        hiddens.append(hidden)
        gate_backs.append(gate_back)
        up_backs.append(up_back)
    normed_two_grad = group.collect(back_chunks)
    groups = [(normed_chunks, [gate_backs, up_backs]), (grad_chunks, [hiddens])]
    if gate_weight.shape[1] % 128:
        ffn_grads = jnp.concatenate(
            [
                sum(turn(*pair) for pair in zip(lefts, right)).astype(BF16)
                for lefts, rights in groups
                for right in rights
            ],
            axis=1,
        )
    else:
        ffn_grads = weight_grads(groups)
    ffn_sums = lax.psum_scatter(ffn_grads, "fsdp", scatter_dimension=0, tiled=True)
    inner_grad, gain_two_grad = norm_back(hidden_one, gains[1], normed_two_grad)
    hidden_one_grad = out_grad.astype(F32) + inner_grad
    branch_own = hidden_one_grad.astype(BF16)
    if special:
        w_out_other = gather_one(group.swap(output_weight.T))
        combined_grads = [
            matmul(branch_own, w_out),
            group.swap(matmul(branch_own, w_out_other).astype(BF16)),
        ]
        attended_grad, gate_pre_grad, recalled_grad, branch_own, ffn_other, _ = open_grads(
            group.rank, combined_grads, gate_pre, recalled,
            [branch_own, ffn[1].astype(BF16), ffn_grads],
        )
        branch_rows = group.ordered([branch_own, group.swap(branch_own)])
        ffn = [ffn[0], ffn_other]
    else:
        branch_rows = group.ordered(group.spread(branch_own))
        attended_grad, gate_pre_grad, recalled_grad = open_grads(
            group.rank, [matmul(branch_rows, w_out)], gate_pre, recalled, []
        )
    output = (hidden_one + group.collect(ffn)).astype(BF16)
    query_mem, key_mem, value_mem, init_grad = memory_backward(
        queries, key_rows, value_rows, live, span_starts, memory_rates, recalled_grad, states
    )
    query_back, key_back, value_back, persist_grad = attention_backward(
        queries, key_rows, value_rows, persist, doc_ids, logs, attended_grad,
        query_mem, key_mem, value_mem,
    )
    backs = [query_back, key_back, value_back, gate_pre_grad]
    half = tokens.shape[0]
    if group.size == 2:
        other = project_back((1 - group.rank) * (half // TILE), half, backs, packed, BF16)
        own = project_back(group.rank * (half // TILE), half, backs, packed, F32)
        normed_grad = own + group.swap(other).astype(F32)
    else:
        normed_grad = group.collect(
            [project_back(jnp.int32(0), half * group.size, backs, packed, BF16)]
        )
    small = [init_grad.T.reshape(depth, -1), persist_grad.reshape(depth, -1)]
    widths = [width] * 5 + [piece.shape[1] for piece in small]
    spare = -sum(widths) % 128
    small = jnp.concatenate(small + [jnp.zeros((depth, spare), F32)], axis=1).astype(BF16)
    pairs = [([normed_all], [[back] for back in backs]), ([branch_rows], [[combined]])]
    if special:
        sums = ring_scatter(*weight_grads(pairs, small, lax.axis_index("fsdp") % 2))
    else:
        sums = lax.psum_scatter(
            weight_grads(pairs, small), "fsdp", scatter_dimension=0, tiled=True
        ).astype(F32)
    query_out, key_out, value_out, mix_out, out_weight_out, init_out, persist_out = split_columns(
        sums, widths
    )
    gate_out, up_out, down_out = split_columns(
        ffn_sums.astype(F32), [gate_weight.shape[1]] * 3
    )
    input_grad, gain_one_grad = norm_back(rows_in, gains[0], normed_grad)
    tokens_grad = (hidden_one_grad + input_grad).astype(BF16)
    gain_terms = jnp.stack([gain_one_grad, gain_two_grad]).reshape(2, fsdp, local)
    gain_terms = lax.all_to_all(gain_terms.transpose(1, 0, 2), "fsdp", 0, 0, tiled=True)
    gains_grad = lax.psum(jnp.sum(gain_terms, axis=0), "tp")
    return (
        output,
        tokens_grad,
        gains_grad,
        query_out,
        key_out,
        value_out,
        mix_out,
        out_weight_out.T,
        persist_out.reshape(persistent_tokens.shape),
        init_out.reshape(-1, width).T,
        gate_out,
        up_out,
        down_out.T,
    )


def solution(mesh):
    placed = (
        P(("fsdp", "tp"), None),
        P(None, "fsdp"),
        P("fsdp", "tp"),
        P("fsdp", "tp"),
        P("fsdp", "tp"),
        P("fsdp", "tp"),
        P("tp", "fsdp"),
        P("fsdp", "tp"),
        P("tp", "fsdp"),
        P("fsdp", "tp"),
        P("fsdp", "tp"),
        P("tp", "fsdp"),
        P("fsdp"),
        P("fsdp"),
        P(None, "fsdp", "tp"),
        P(("fsdp", "tp"), None),
    )
    return jax.shard_map(
        on_device,
        mesh=mesh,
        in_specs=placed,
        out_specs=(
            P(("fsdp", "tp"), None),
            P(("fsdp", "tp"), None),
            P(None, "fsdp"),
            P("fsdp", "tp"),
            P("fsdp", "tp"),
            P("fsdp", "tp"),
            P("fsdp", "tp"),
            P("tp", "fsdp"),
            P("fsdp", "tp"),
            P("tp", "fsdp"),
            P("fsdp", "tp"),
            P("fsdp", "tp"),
            P("tp", "fsdp"),
        ),
        check_vma=False,
    )
```

```python
import functools
import jax, jax.numpy as jnp
from jax import lax
from jax.experimental import pallas as pl
from jax.experimental.pallas import tpu as pltpu
from jax.sharding import PartitionSpec as P

HEAD = 128
SPAN = 64
SEQ_LEN = 1024
BF16 = jnp.bfloat16
F32 = jnp.float32
NN = (((1,), (0,)), ((), ()))
NT = (((1,), (1,)), ((), ()))
TN = (((0,), (0,)), ((), ()))


def dot(left, right, dims=NN):
    return lax.dot_general(left, right, dims, preferred_element_type=F32)


def sigmoid(values):
    return 0.5 * jnp.tanh(0.5 * values) + 0.5


def cost(microseconds, nbytes):
    return pl.CostEstimate(
        flops=int(microseconds * 1e9), bytes_accessed=int(nbytes), transcendentals=0
    )


def memory_forward_kernel(
    unroll, sequences, heads, starts_ref, rates_ref, queries_ref, keys_ref, values_ref, live_ref,
    init_ref, recalled_ref, states_ref, first_ref, second_ref, moment_one_ref, moment_two_ref,
):
    spans = SEQ_LEN // SPAN
    step = pl.program_id(0)
    chains = [(s, h) for s in range(sequences) for h in range(heads)]

    @pl.when(step == 0)
    def _():
        for place, (s, h) in enumerate(chains):
            first_ref[place] = jnp.zeros((HEAD, HEAD), F32)
            second_ref[place] = jnp.zeros((HEAD, HEAD), F32)
            moment_one_ref[place] = jnp.zeros((HEAD, HEAD), F32)
            moment_two_ref[place] = jnp.zeros((HEAD, HEAD), F32)

    state = [
        (first_ref[i], second_ref[i], moment_one_ref[i], moment_two_ref[i])
        for i in range(len(chains))
    ]
    for part in range(unroll):
        rows = pl.ds(part * SPAN, SPAN)
        span = step * unroll + part
        begins = [starts_ref[s * spans + span] != 0 for s in range(sequences)]
        used = []
        for place, (s, h) in enumerate(chains):
            one, two, moment_one, moment_two = state[place]
            start = init_ref[pl.ds(h * HEAD, HEAD), :]
            used.append(
                (
                    jnp.where(begins[s], start[:, :HEAD], one),
                    jnp.where(begins[s], start[:, HEAD:], two),
                    jnp.where(begins[s], 0.0, moment_one),
                    jnp.where(begins[s], 0.0, moment_two),
                )
            )
        low = [(one.astype(BF16), two.astype(BF16)) for one, two, _, _ in used]
        for place in range(len(chains)):
            states_ref[part, place, :, :HEAD] = low[place][0]
            states_ref[part, place, :, HEAD:] = low[place][1]
        cols = [pl.ds(h * HEAD, HEAD) for _, h in chains]
        keys = [keys_ref[s, rows, cols[i]] for i, (s, _) in enumerate(chains)]
        hidden = [dot(keys[i], low[i][0]) for i in range(len(chains))]
        gates = [sigmoid(value) for value in hidden]
        active = [(h * g).astype(BF16) for h, g in zip(hidden, gates)]
        outs = [dot(active[i], low[i][1]) for i in range(len(chains))]
        errors = [
            ((outs[i] - values_ref[s, rows, cols[i]].astype(F32)) * live_ref[s, rows, :]).astype(BF16)
            for i, (s, _) in enumerate(chains)
        ]
        back = [dot(errors[i], low[i][1], NT) for i in range(len(chains))]
        inner = [
            (b * (g * (1.0 + h * (1.0 - g)))).astype(BF16)
            for b, h, g in zip(back, hidden, gates)
        ]
        grad_one = [dot(keys[i], inner[i], TN) for i in range(len(chains))]
        grad_two = [dot(active[i], errors[i], TN) for i in range(len(chains))]
        state = []
        for place, (s, h) in enumerate(chains):
            one, two, moment_one, moment_two = used[place]
            index = (s * spans + span) * heads + h
            stride = sequences * spans * heads
            momentum = rates_ref[index]
            size = rates_ref[stride + index]
            keep = 1.0 - rates_ref[2 * stride + index]
            moment_one = momentum * moment_one - size * grad_one[place]
            moment_two = momentum * moment_two - size * grad_two[place]
            state.append((keep * one + moment_one, keep * two + moment_two, moment_one, moment_two))
        for place, (s, h) in enumerate(chains):
            asked = dot(queries_ref[s, rows, cols[place]], low[place][0])
            asked = (asked * sigmoid(asked)).astype(BF16)
            recalled_ref[s, rows, cols[place]] = dot(asked, low[place][1]).astype(recalled_ref.dtype)
    for place in range(len(chains)):
        first_ref[place], second_ref[place], moment_one_ref[place], moment_two_ref[place] = state[place]


def memory_forward(queries, key_rows, value_rows, live, starts, rates, init, unroll=2):
    rows, width = queries.shape
    sequences, heads = rows // SEQ_LEN, width // HEAD
    spans = SEQ_LEN // SPAN
    chains = sequences * heads

    def by_seq(values):
        return values.reshape(sequences, SEQ_LEN, width)

    block = pl.BlockSpec((sequences, unroll * SPAN, width), lambda c: (0, c, 0))
    smem = pl.BlockSpec(memory_space=pltpu.SMEM)
    recalled, states = pl.pallas_call(
        functools.partial(memory_forward_kernel, unroll, sequences, heads),
        grid=(spans // unroll,),
        in_specs=[
            smem, smem, block, block, block,
            pl.BlockSpec((sequences, unroll * SPAN, 1), lambda c: (0, c, 0)),
            pl.BlockSpec((heads * HEAD, 2 * HEAD), lambda c: (0, 0)),
        ],
        out_specs=[
            block,
            pl.BlockSpec((unroll, chains, HEAD, 2 * HEAD), lambda c: (c, 0, 0, 0)),
        ],
        out_shape=[
            jax.ShapeDtypeStruct((sequences, SEQ_LEN, width), F32),
            jax.ShapeDtypeStruct((spans, chains, HEAD, 2 * HEAD), BF16),
        ],
        scratch_shapes=[pltpu.VMEM((chains, HEAD, HEAD), F32)] * 4,
        cost_estimate=cost(14, 0),
        name="memory_forward",
    )(
        starts, rates.reshape(-1), by_seq(queries), by_seq(key_rows), by_seq(value_rows),
        live.reshape(sequences, SEQ_LEN, 1), init,
    )
    return recalled.reshape(rows, width), states


def memory_backward_kernel(
    unroll, sequences, heads, starts_ref, rates_ref, queries_ref, keys_ref, values_ref, live_ref,
    grads_ref, states_ref, query_out, key_out, value_out, init_out,
    first_ref, second_ref, moment_one_ref, moment_two_ref, total_ref,
):
    spans = SEQ_LEN // SPAN
    step = pl.program_id(0)
    chains = [(s, h) for s in range(sequences) for h in range(heads)]
    count = len(chains)
    zero = jnp.zeros((HEAD, HEAD), F32)

    @pl.when(step == 0)
    def _():
        for i in range(count):
            first_ref[i] = zero
            second_ref[i] = zero
            moment_one_ref[i] = zero
            moment_two_ref[i] = zero
            total_ref[i] = jnp.zeros((HEAD, 2 * HEAD), F32)

    state = [(first_ref[i], second_ref[i], moment_one_ref[i], moment_two_ref[i]) for i in range(count)]
    cols = [pl.ds(h * HEAD, HEAD) for _, h in chains]
    for part in reversed(range(unroll)):
        rows = pl.ds(part * SPAN, SPAN)
        span = spans - (step + 1) * unroll + part
        stride = sequences * spans * heads
        each = range(count)
        one = [states_ref[part, i, :, :HEAD] for i in each]
        two = [states_ref[part, i, :, HEAD:] for i in each]
        queries = [queries_ref[chains[i][0], rows, cols[i]] for i in each]
        keys = [keys_ref[chains[i][0], rows, cols[i]] for i in each]
        values = [values_ref[chains[i][0], rows, cols[i]].astype(F32) for i in each]
        live = [live_ref[chains[i][0], rows, :] for i in each]
        grads = [grads_ref[chains[i][0], rows, cols[i]].astype(BF16) for i in each]
        hidden = [dot(keys[i], one[i]) for i in each]
        gates = [sigmoid(hidden[i]) for i in each]
        active = [(hidden[i] * gates[i]).astype(BF16) for i in each]
        errors = [((dot(active[i], two[i]) - values[i]) * live[i]).astype(BF16) for i in each]
        back = [dot(errors[i], two[i], NT) for i in each]
        slope = [gates[i] * (1.0 + hidden[i] * (1.0 - gates[i])) for i in each]
        bend = [
            gates[i] * (1.0 - gates[i]) * (2.0 + hidden[i] * (1.0 - 2.0 * gates[i])) * back[i]
            for i in each
        ]
        inner = [(back[i] * slope[i]).astype(BF16) for i in each]
        asked = [dot(queries[i], one[i]) for i in each]
        asked_gate = [sigmoid(asked[i]) for i in each]
        asked_active = [(asked[i] * asked_gate[i]).astype(BF16) for i in each]
        asked_grad = [
            (
                dot(grads[i], two[i], NT)
                * (asked_gate[i] * (1.0 + asked[i] * (1.0 - asked_gate[i])))
            ).astype(BF16)
            for i in each
        ]
        for i in each:
            query_out[chains[i][0], rows, cols[i]] = dot(asked_grad[i], one[i], NT)
        momentum, size, keep = [], [], []
        for s, h in chains:
            index = (s * spans + span) * heads + h
            momentum.append(rates_ref[index])
            size.append(rates_ref[stride + index])
            keep.append(1.0 - rates_ref[2 * stride + index])
        sum_one = [state[i][0] + state[i][2] for i in each]
        sum_two = [state[i][1] + state[i][3] for i in each]
        step_one = [(-size[i] * sum_one[i]).astype(BF16) for i in each]
        step_two = [(-size[i] * sum_two[i]).astype(BF16) for i in each]
        inner_grad = [dot(keys[i], step_one[i]) for i in each]
        back_grad = [(inner_grad[i] * slope[i]).astype(BF16) for i in each]
        error_grad = [
            (dot(back_grad[i], two[i]) + dot(active[i], step_two[i])) * live[i] for i in each
        ]
        for i in each:
            value_out[chains[i][0], rows, cols[i]] = -error_grad[i]
        out_grad = [error_grad[i].astype(BF16) for i in each]
        active_grad = [dot(errors[i], step_two[i], NT) + dot(out_grad[i], two[i], NT) for i in each]
        hidden_grad = [
            (active_grad[i] * slope[i] + inner_grad[i] * bend[i]).astype(BF16) for i in each
        ]
        new_one = [
            keep[i] * state[i][0] + dot(keys[i], hidden_grad[i], TN) + dot(queries[i], asked_grad[i], TN)
            for i in each
        ]
        new_two = [
            keep[i] * state[i][1]
            + dot(back_grad[i], errors[i], TN)
            + dot(active[i], out_grad[i], TN)
            + dot(asked_active[i], grads[i], TN)
            for i in each
        ]
        for i in each:
            key_out[chains[i][0], rows, cols[i]] = dot(inner[i], step_one[i], NT) + dot(
                hidden_grad[i], one[i], NT
            )
        begins = [starts_ref[s * spans + span] != 0 for s in range(sequences)]
        state = []
        for i, (s, h) in enumerate(chains):
            begin = begins[s]
            total_ref[i, :, :HEAD] += jnp.where(begin, new_one[i], 0.0)
            total_ref[i, :, HEAD:] += jnp.where(begin, new_two[i], 0.0)
            state.append(
                (
                    jnp.where(begin, 0.0, new_one[i]),
                    jnp.where(begin, 0.0, new_two[i]),
                    jnp.where(begin, 0.0, momentum[i] * sum_one[i]),
                    jnp.where(begin, 0.0, momentum[i] * sum_two[i]),
                )
            )
    for i in range(count):
        first_ref[i], second_ref[i], moment_one_ref[i], moment_two_ref[i] = state[i]

    @pl.when(step == pl.num_programs(0) - 1)
    def _():
        for h in range(heads):
            whole = sum(total_ref[s * heads + h] for s in range(sequences))
            init_out[pl.ds(h, 2 * HEAD, stride=heads), :] = whole.T


def memory_backward(
    queries, key_rows, value_rows, live, starts, rates, grads, states, unroll=2
):
    rows, width = queries.shape
    sequences, heads = rows // SEQ_LEN, width // HEAD
    spans = SEQ_LEN // SPAN
    chains = sequences * heads
    steps = spans // unroll

    def by_seq(values):
        return values.reshape(sequences, SEQ_LEN, width)

    block = pl.BlockSpec((sequences, unroll * SPAN, width), lambda c: (0, steps - 1 - c, 0))
    smem = pl.BlockSpec(memory_space=pltpu.SMEM)
    shape = jax.ShapeDtypeStruct((sequences, SEQ_LEN, width), F32)
    query_mem, key_mem, value_mem, init_grad = pl.pallas_call(
        functools.partial(memory_backward_kernel, unroll, sequences, heads),
        grid=(steps,),
        in_specs=[
            smem, smem, block, block, block,
            pl.BlockSpec((sequences, unroll * SPAN, 1), lambda c: (0, steps - 1 - c, 0)),
            block,
            pl.BlockSpec((unroll, chains, HEAD, 2 * HEAD), lambda c: (steps - 1 - c, 0, 0, 0)),
        ],
        out_specs=[
            block, block, block,
            pl.BlockSpec((2 * HEAD * heads, HEAD), lambda c: (0, 0)),
        ],
        out_shape=[
            shape, shape, shape,
            jax.ShapeDtypeStruct((2 * HEAD * heads, HEAD), F32),
        ],
        scratch_shapes=[pltpu.VMEM((chains, HEAD, HEAD), F32)] * 4
        + [pltpu.VMEM((chains, HEAD, 2 * HEAD), F32)],
        cost_estimate=cost(27, 0),
        name="memory_backward",
    )(
        starts, rates.reshape(-1), by_seq(queries), by_seq(key_rows), by_seq(value_rows),
        live.reshape(sequences, SEQ_LEN, 1), by_seq(grads), states,
    )
    return tuple(x.reshape(rows, width) for x in (query_mem, key_mem, value_mem)) + (init_grad,)

PERSIST = 16
TILE = 256
MASKED_SCORE = -1e30
SCALING = HEAD ** (-0.5)


def masked_scores(tile, queries, keys_ref, column_ref, row_ref):
    reach = (tile + 1) * TILE
    scores = dot(keys_ref[0, :reach, :], queries, NT) * SCALING
    same = column_ref[0, :reach, :] == row_ref[0, :, tile * TILE : reach]
    if tile:
        early = jnp.where(same[: tile * TILE], scores[: tile * TILE], MASKED_SCORE)
    own = same[tile * TILE :] & (
        lax.broadcasted_iota(jnp.int32, (TILE, TILE), 0)
        <= lax.broadcasted_iota(jnp.int32, (TILE, TILE), 1)
    )
    own = jnp.where(own, scores[tile * TILE :], MASKED_SCORE)
    return jnp.concatenate([early, own], axis=0) if tile else own


def attention_forward_kernel(
    queries_ref, keys_ref, values_ref, persist_ref, column_ref, row_ref, gate_ref, recalled_ref,
    after_ref, combined_ref, log_ref,
):
    values_t = values_ref[0].T
    fixed_keys = persist_ref[:PERSIST, :].astype(BF16)
    fixed_values_t = persist_ref[PERSIST:, :].astype(F32).T.astype(BF16)
    for tile in range(SEQ_LEN // TILE):
        rows = slice(tile * TILE, (tile + 1) * TILE)
        reach = (tile + 1) * TILE
        queries = queries_ref[0, rows, :]
        scores = masked_scores(tile, queries, keys_ref, column_ref, row_ref)
        fixed = dot(fixed_keys, queries, NT) * SCALING
        highest = jnp.maximum(
            jnp.max(scores, axis=0, keepdims=True), jnp.max(fixed, axis=0, keepdims=True)
        )
        weights = jnp.exp(scores - highest)
        fixed_weights = jnp.exp(fixed - highest)
        totals = jnp.sum(weights, axis=0, keepdims=True) + jnp.sum(
            fixed_weights, axis=0, keepdims=True
        )
        part = 1.0 / totals
        attended = dot(values_t[:, :reach], (weights * part).astype(BF16)) + dot(
            fixed_values_t, (fixed_weights * part).astype(BF16)
        )
        log_ref[0, 0, :, rows] = highest + jnp.log(totals)
        combined_ref[0, rows, :] = (
            attended.T + sigmoid(gate_ref[0, rows, :]) * recalled_ref[0, rows, :]
        ).astype(BF16)


def attention_forward(
    queries, key_rows, value_rows, persist, documents, gate_pre, recalled, after
):
    rows, width = queries.shape
    sequences, heads = rows // SEQ_LEN, width // HEAD

    def by_seq(values):
        return values.reshape(sequences, SEQ_LEN, width)

    block = pl.BlockSpec((1, SEQ_LEN, HEAD), lambda h, s: (s, 0, h))
    combined, logs = pl.pallas_call(
        attention_forward_kernel,
        grid=(heads, sequences),
        in_specs=[
            block, block, block,
            pl.BlockSpec((2 * PERSIST, HEAD), lambda h, s: (0, h)),
            pl.BlockSpec((1, SEQ_LEN, 1), lambda h, s: (s, 0, 0)),
            pl.BlockSpec((1, 1, SEQ_LEN), lambda h, s: (s, 0, 0)),
            block, block, pl.BlockSpec(memory_space=pl.ANY),
        ],
        out_specs=[block, pl.BlockSpec((1, 1, 1, SEQ_LEN), lambda h, s: (s, h, 0, 0))],
        out_shape=[
            jax.ShapeDtypeStruct((sequences, SEQ_LEN, width), BF16),
            jax.ShapeDtypeStruct((sequences, heads, 1, SEQ_LEN), F32),
        ],
        cost_estimate=cost(12, 0),
        name="attention_forward",
    )(
        by_seq(queries), by_seq(key_rows), by_seq(value_rows), persist,
        documents.reshape(sequences, SEQ_LEN, 1), documents.reshape(sequences, 1, SEQ_LEN),
        by_seq(gate_pre), by_seq(recalled), after,
    )
    return combined.reshape(rows, width), logs


def attention_backward_kernel(
    queries_ref, keys_ref, values_ref, persist_ref, column_ref, row_ref, log_ref, grad_ref,
    query_mem_ref, key_mem_ref, value_mem_ref,
    query_out, key_out, value_out, persist_out, key_total, value_total,
):
    keys_t = keys_ref[0].T
    fixed_keys = persist_ref[:PERSIST, :].astype(BF16)
    fixed_values = persist_ref[PERSIST:, :].astype(BF16)
    fixed_keys_t = fixed_keys.astype(F32).T.astype(BF16)

    @pl.when(pl.program_id(1) == 0)
    def _():
        persist_out[...] = jnp.zeros(persist_out.shape, F32)

    for tile in reversed(range(SEQ_LEN // TILE)):
        rows = slice(tile * TILE, (tile + 1) * TILE)
        reach = (tile + 1) * TILE
        queries = queries_ref[0, rows, :]
        grads = grad_ref[0, rows, :]
        logs = log_ref[0, 0, :, rows]
        scores = masked_scores(tile, queries, keys_ref, column_ref, row_ref)
        prob = jnp.exp(scores - logs)
        fixed_prob = jnp.exp(dot(fixed_keys, queries, NT) * SCALING - logs)
        prob_grad = dot(values_ref[0, :reach, :], grads, NT)
        fixed_prob_grad = dot(fixed_values, grads, NT)
        inner = jnp.sum(prob * prob_grad, axis=0, keepdims=True) + jnp.sum(
            fixed_prob * fixed_prob_grad, axis=0, keepdims=True
        )
        score_grad = (prob * (prob_grad - inner)).astype(BF16)
        fixed_score_grad = (fixed_prob * (fixed_prob_grad - inner)).astype(BF16)
        key_part = dot(score_grad, queries)
        value_part = dot(prob.astype(BF16), grads)
        if tile == SEQ_LEN // TILE - 1:
            key_total[...] = key_part
            value_total[...] = value_part
        else:
            key_total[:reach, :] += key_part
            value_total[:reach, :] += value_part
        persist_out[:PERSIST, :] += SCALING * dot(fixed_score_grad, queries)
        persist_out[PERSIST:, :] += dot(fixed_prob.astype(BF16), grads)
        query_part = dot(keys_t[:, :reach], score_grad) + dot(fixed_keys_t, fixed_score_grad)
        query_out[0, rows, :] = (SCALING * query_part.T + query_mem_ref[0, rows, :]).astype(BF16)
    key_out[0] = (SCALING * key_total[...] + key_mem_ref[0]).astype(BF16)
    value_out[0] = (value_total[...] + value_mem_ref[0]).astype(BF16)


def attention_backward(
    queries, key_rows, value_rows, persist, documents, logs, attended_grad,
    query_mem, key_mem, value_mem,
):
    rows, width = queries.shape
    sequences, heads = rows // SEQ_LEN, width // HEAD

    def by_seq(values):
        return values.reshape(sequences, SEQ_LEN, width)

    block = pl.BlockSpec((1, SEQ_LEN, HEAD), lambda h, s: (s, 0, h))
    fixed = pl.BlockSpec((2 * PERSIST, HEAD), lambda h, s: (0, h))
    shape = jax.ShapeDtypeStruct((sequences, SEQ_LEN, width), BF16)
    query_back, key_back, value_back, persist_grad = pl.pallas_call(
        attention_backward_kernel,
        grid=(heads, sequences),
        in_specs=[
            block, block, block, fixed,
            pl.BlockSpec((1, SEQ_LEN, 1), lambda h, s: (s, 0, 0)),
            pl.BlockSpec((1, 1, SEQ_LEN), lambda h, s: (s, 0, 0)),
            pl.BlockSpec((1, 1, 1, SEQ_LEN), lambda h, s: (s, h, 0, 0)),
            block, block, block, block,
        ],
        out_specs=[block, block, block, fixed],
        out_shape=[shape, shape, shape, jax.ShapeDtypeStruct((2 * PERSIST, width), F32)],
        scratch_shapes=[pltpu.VMEM((SEQ_LEN, HEAD), F32)] * 2,
        cost_estimate=cost(15, 0),
        name="attention_backward",
    )(
        by_seq(queries), by_seq(key_rows), by_seq(value_rows), persist,
        documents.reshape(sequences, SEQ_LEN, 1), documents.reshape(sequences, 1, SEQ_LEN),
        logs, by_seq(attended_grad), by_seq(query_mem), by_seq(key_mem), by_seq(value_mem),
    )
    return tuple(x.reshape(rows, width) for x in (query_back, key_back, value_back)) + (persist_grad,)


EPSILON = 1e-05


def turn(left, right):
    return lax.dot_general(left, right, TN, preferred_element_type=F32)


def matmul(left, right):
    return lax.dot_general(left, right, NN, preferred_element_type=F32)


def matmul_right(left, right):
    return lax.dot_general(left, right, NT, preferred_element_type=F32)


def rms_norm(values, gain):
    return values * lax.rsqrt(jnp.mean(values * values, axis=-1, keepdims=True) + EPSILON) * gain


def norm_back(values, gain, grads):
    scale = lax.rsqrt(jnp.mean(values * values, axis=-1, keepdims=True) + EPSILON)
    weighted = grads * gain
    inner = jnp.mean(values * weighted, axis=-1, keepdims=True)
    return scale * weighted - values * (scale * scale * scale * inner), jnp.sum(
        grads * values * scale, axis=0
    )


def project_kernel(
    halves, half_tiles, rank_ref, gains_ref, *refs
):
    token_refs = refs[:halves]
    weight_ref, normed_out, query_out, key_out, value_out, gate_out = refs[halves:]
    width = query_out.shape[1]
    rows = token_refs[0][...]
    if halves == 2:
        mine = pl.program_id(0) // half_tiles == rank_ref[0]
        rows = jnp.where(mine, rows, token_refs[1][...])
    rows = rows.astype(F32)
    normed = rms_norm(rows, gains_ref[...]).astype(BF16)
    normed_out[...] = normed
    for place, out in enumerate((query_out, key_out, value_out, gate_out)):
        out[...] = dot(normed, weight_ref[:, place * width : (place + 1) * width]).astype(out.dtype)


def project(rank, gain, chunks, weights, width):
    halves = len(chunks)
    depth = chunks[0].shape[1]
    half_tiles = chunks[0].shape[0] // TILE
    rows = halves * chunks[0].shape[0]

    out = pl.BlockSpec((TILE, width), lambda i, rank_ref: (i, 0))
    shape = jax.ShapeDtypeStruct((rows, width), BF16)
    return pl.pallas_call(
        functools.partial(project_kernel, halves, half_tiles),
        grid_spec=pltpu.PrefetchScalarGridSpec(
            num_scalar_prefetch=1,
            grid=(rows // TILE,),
            in_specs=[pl.BlockSpec((1, depth), lambda i, rank_ref: (0, 0))]
            + [
                pl.BlockSpec((TILE, depth), chunk_map(place, half_tiles, halves))
                for place in range(halves)
            ]
            + [
                pl.BlockSpec(
                    (depth, 4 * width), lambda i, rank_ref: (0, 0), pipeline_mode=pl.Buffered(1)
                )
            ],
            out_specs=[pl.BlockSpec((TILE, depth), lambda i, rank_ref: (i, 0))] + [out] * 4,
        ),
        out_shape=[jax.ShapeDtypeStruct((rows, depth), BF16)]
        + [shape] * 3
        + [jax.ShapeDtypeStruct((rows, width), F32)],
        cost_estimate=cost(8, 0),
        name="project",
    )(rank.reshape(1), gain.reshape(1, -1), *chunks, weights)


def project_back_kernel(base_ref, *refs):
    weight_ref, out_ref = refs[-2:]
    width = refs[0].shape[1]
    total = 0.0
    for place, back in enumerate(refs[:-2]):
        total += dot(back[...], weight_ref[:, place * width : (place + 1) * width], NT)
    out_ref[...] = total.astype(out_ref.dtype)


def project_back(base, rows, backs, weights, dtype):
    width = backs[0].shape[1]
    depth = weights.shape[0]
    return pl.pallas_call(
        project_back_kernel,
        grid_spec=pltpu.PrefetchScalarGridSpec(
            num_scalar_prefetch=1,
            grid=(rows // TILE,),
            in_specs=[pl.BlockSpec((TILE, width), lambda i, base_ref: (base_ref[0] + i, 0))] * 4
            + [
                pl.BlockSpec(
                    (depth, 4 * width), lambda i, base_ref: (0, 0), pipeline_mode=pl.Buffered(1)
                )
            ],
            out_specs=pl.BlockSpec((TILE, depth), lambda i, base_ref: (i, 0)),
        ),
        out_shape=jax.ShapeDtypeStruct((rows, depth), dtype),
        cost_estimate=cost(4, 0),
        name="project_back",
    )(jnp.reshape(base, (1,)).astype(jnp.int32), *backs, weights)


def weight_grads_kernel(counts, extra, split, core_ref, *refs):
    at = 0
    parts = []
    for chunk_count, right_count in counts:
        lefts = [ref[...] for ref in refs[at : at + chunk_count]]
        at += chunk_count
        for _ in range(right_count):
            parts.append(
                sum(
                    dot(left, right[...], TN)
                    for left, right in zip(lefts, refs[at : at + chunk_count])
                ).astype(BF16)
            )
            at += chunk_count
    if extra and split:
        parts.append(refs[at][...].astype(BF16))
        lines, persist_ref = refs[-1], refs[at + 1]
        heads = persist_ref.shape[1] // HEAD
        lines[...] = jnp.zeros(lines.shape, F32)
        for row in range(2):
            for h in range(heads):
                for device in range(4):
                    spot = device * (TILE // 4) + row * heads + h
                    lines[spot : spot + 1, :] = persist_ref[
                        2 * device + row : 2 * device + row + 1, h * HEAD : (h + 1) * HEAD
                    ]
        parts.append(lines[...].astype(BF16))
    elif extra:
        parts.append(refs[at][...])
    outs = refs[at + extra :]
    place = 0
    for part in parts:
        cols = slice(place, place + part.shape[1])
        place += part.shape[1]
        if split:
            local = part.shape[0] // 4
            for y in range(2):
                even = part[2 * y * local : (2 * y + 1) * local]
                odd = part[(2 * y + 1) * local : (2 * y + 2) * local]
                first = core_ref[0] == 0
                outs[0][y, :, cols] = jnp.where(first, even, odd)
                outs[1][y, :, cols] = jnp.where(first, odd, even)
        else:
            outs[0][:, cols] = part


def weight_grads(groups, extra=(), core=None):
    depth = groups[0][0][0].shape[1]
    rights = [right for _, group in groups for right in group]
    total = sum(right[0].shape[1] for right in rights) + (
        2 * HEAD if core is not None else sum(piece.shape[1] for piece in extra)
    )
    operands, specs, counts = [], [], []
    for lefts, group in groups:
        counts.append((len(lefts), len(group)))
        for left in lefts:
            operands.append(left)
            specs.append(pl.BlockSpec((left.shape[0], TILE), lambda d, core_ref: (0, d)))
        for right in group:
            for chunk in right:
                operands.append(chunk)
                specs.append(
                    pl.BlockSpec(
                        chunk.shape, lambda d, core_ref: (0, 0), pipeline_mode=pl.Buffered(1)
                    )
                )
    if core is not None:
        specs.append(pl.BlockSpec((TILE, HEAD), lambda d, core_ref: (d, 0)))
        specs.append(pl.BlockSpec((8, extra[1].shape[1]), lambda d, core_ref: (d, 0)))
    elif extra:
        specs.append(pl.BlockSpec((TILE, extra[0].shape[1]), lambda d, core_ref: (d, 0)))
    operands.extend(extra)
    if core is None:
        out_specs = pl.BlockSpec((TILE, total), lambda d, core_ref: (d, 0))
        out_shape = jax.ShapeDtypeStruct((depth, total), BF16)
    else:
        out_specs = [pl.BlockSpec((2, TILE // 4, total), lambda d, core_ref: (d, 0, 0))] * 2
        out_shape = [jax.ShapeDtypeStruct((depth * 2 // TILE, TILE // 4, total), BF16)] * 2
    return pl.pallas_call(
        functools.partial(weight_grads_kernel, tuple(counts), len(extra), core is not None),
        grid_spec=pltpu.PrefetchScalarGridSpec(
            num_scalar_prefetch=1,
            grid=(depth // TILE,),
            in_specs=specs,
            out_specs=out_specs,
            scratch_shapes=[] if core is None else [pltpu.VMEM((TILE, HEAD), F32)],
        ),
        out_shape=out_shape,
        cost_estimate=cost(total * 3e-3, 0),
        name="weight_grads",
    )(jnp.reshape(0 if core is None else core, (1,)).astype(jnp.int32), *operands)


def pack_first_kernel(
    query_ref, key_ref, value_ref, mix_ref, init_ref, persist_ref, gains_ref, out_ref, init_rows
):
    local, width = query_ref.shape
    for place, ref in enumerate((query_ref, key_ref, value_ref, mix_ref)):
        out_ref[:, place * width : (place + 1) * width] = ref[...]
    heads = width // HEAD
    columns = init_ref.shape[1]
    for h in range(heads):
        init_rows[pl.ds(h, columns, stride=heads), :] = (
            init_ref[pl.ds(h * HEAD, HEAD), :].astype(F32).T
        )
    out_ref[:, 4 * width : 4 * width + HEAD] = init_rows[...].astype(BF16)
    init_rows[...] = jnp.zeros(init_rows.shape, F32)
    for row in range(persist_ref.shape[0]):
        for h in range(heads):
            at = row * heads + h
            init_rows[at : at + 1, :] = persist_ref[
                row : row + 1, h * HEAD : (h + 1) * HEAD
            ].astype(F32)
    gain_row = persist_ref.shape[0] * heads
    init_rows[gain_row : gain_row + 2, :local] = gains_ref[...].astype(F32)
    out_ref[:, 4 * width + HEAD :] = init_rows[...].astype(BF16)


def pack_first(query, key, value, mix, init, persist, gains):
    local, width = query.shape
    return pl.pallas_call(
        pack_first_kernel,
        out_shape=jax.ShapeDtypeStruct((local, 4 * width + 2 * HEAD), BF16),
        scratch_shapes=[pltpu.VMEM((local, HEAD), F32)],
        cost_estimate=cost(2, 0),
        name="pack_first",
    )(query, key, value, mix, init, persist, gains)


def project_pieces_kernel(half_tiles, starts_ref, own_ref, other_ref, *refs):
    pieces = refs[:16]
    (
        weight_out, normed_out, query_out, key_out, value_out, gate_out, gains_out, persist_out,
        init_out, first_rows, second_rows, pair_rows,
    ) = refs[16:]
    width = query_out.shape[1]
    heads = width // HEAD
    local = pieces[0].shape[0]

    @pl.when(pl.program_id(0) == 0)
    def _():
        for place, piece in enumerate(pieces):
            rows = pl.ds(pl.multiple_of(starts_ref[place], local), local)
            weight_out[rows, :] = piece[:, : 4 * width]
            first_rows[rows, :] = piece[:, 4 * width : 4 * width + HEAD].astype(F32)
            second_rows[rows, :] = piece[:, 4 * width + HEAD :].astype(F32)
        for device in range(16):
            at = device * local + 2 * heads
            gains_out[:, device * local : (device + 1) * local] = second_rows[at : at + 2, :local]
        for h in range(heads):
            for row in range(2):
                pair_rows[pl.ds(row, 16, stride=2), :] = second_rows[
                    pl.ds(row * heads + h, 16, stride=local), :
                ]
            persist_out[:, h * HEAD : (h + 1) * HEAD] = pair_rows[...]
        for h in range(heads):
            init_out[pl.ds(h * HEAD, HEAD), :] = first_rows[pl.ds(h, 2 * HEAD, stride=heads), :].T

    mine = pl.program_id(0) // half_tiles == starts_ref[16]
    rows = jnp.where(mine, own_ref[...], other_ref[...]).astype(F32)
    normed = rms_norm(rows, gains_out[0:1, :]).astype(BF16)
    normed_out[...] = normed
    for place, out in enumerate((query_out, key_out, value_out, gate_out)):
        out[...] = dot(normed, weight_out[:, place * width : (place + 1) * width]).astype(out.dtype)


def project_pieces(starts, chunks, pieces, width):
    depth = chunks[0].shape[1]
    half_tiles = chunks[0].shape[0] // TILE
    rows = 2 * chunks[0].shape[0]

    def chunk(place):
        def index(i, starts_ref):
            start = (starts_ref[16] if place == 0 else 1 - starts_ref[16]) * half_tiles
            return jnp.clip(i - start, 0, half_tiles - 1), 0

        return pl.BlockSpec((TILE, depth), index)

    def whole(shape, **more):
        return pl.BlockSpec(shape, lambda i, starts_ref: (0, 0), **more)

    out = pl.BlockSpec((TILE, width), lambda i, starts_ref: (i, 0))
    shape = jax.ShapeDtypeStruct((rows, width), BF16)
    small = [(2, depth), (2 * PERSIST, width), (width, 2 * HEAD)]
    return pl.pallas_call(
        functools.partial(project_pieces_kernel, half_tiles),
        grid_spec=pltpu.PrefetchScalarGridSpec(
            num_scalar_prefetch=1,
            grid=(rows // TILE,),
            in_specs=[chunk(0), chunk(1)]
            + [whole(piece.shape, pipeline_mode=pl.Buffered(1)) for piece in pieces],
            out_specs=[
                whole((depth, 4 * width)),
                pl.BlockSpec((TILE, depth), lambda i, starts_ref: (i, 0)),
            ]
            + [out] * 4
            + [whole(size) for size in small],
            scratch_shapes=[pltpu.VMEM((depth, HEAD), F32)] * 2
            + [pltpu.VMEM((2 * PERSIST, HEAD), F32)],
        ),
        out_shape=[
            jax.ShapeDtypeStruct((depth, 4 * width), BF16),
            jax.ShapeDtypeStruct((rows, depth), BF16),
        ]
        + [shape] * 3
        + [jax.ShapeDtypeStruct((rows, width), F32)]
        + [jax.ShapeDtypeStruct(size, F32) for size in small],
        cost_estimate=cost(10, 0),
        name="project_pieces",
    )(starts, *chunks, *pieces)


def branch_norm_kernel(after, base_ref, own_ref, got_ref, mine_ref, theirs_ref, rows_ref, gain_ref, *refs):
    hidden_out, normed_out = refs[after:]
    branch = dot(own_ref[...], mine_ref[...], NT) + dot(got_ref[...], theirs_ref[...], NT)
    hidden = rows_ref[...].astype(F32) + branch
    hidden_out[...] = hidden
    normed_out[...] = rms_norm(hidden, gain_ref[...]).astype(BF16)


def branch_norm(base, combined, got, mine, theirs, tokens, gain, after):
    rows, depth = tokens.shape
    width = combined.shape[1]

    def whole(shape):
        return pl.BlockSpec(shape, lambda i, base_ref: (0, 0), pipeline_mode=pl.Buffered(1))

    block = pl.BlockSpec((TILE, depth), lambda i, base_ref: (i, 0))
    return pl.pallas_call(
        functools.partial(branch_norm_kernel, len(after)),
        grid_spec=pltpu.PrefetchScalarGridSpec(
            num_scalar_prefetch=1,
            grid=(rows // TILE,),
            in_specs=[
                pl.BlockSpec((TILE, width), lambda i, base_ref: (base_ref[0] + i, 0)),
                pl.BlockSpec((TILE, width), lambda i, base_ref: (i, 0)),
                whole(mine.shape), whole(theirs.shape), block, whole((1, depth)),
            ]
            + [pl.BlockSpec(memory_space=pl.ANY)] * len(after),
            out_specs=[block, block],
        ),
        out_shape=[
            jax.ShapeDtypeStruct((rows, depth), F32),
            jax.ShapeDtypeStruct((rows, depth), BF16),
        ],
        cost_estimate=cost(4, 0),
        name="branch_norm",
    )(base, combined, got, mine, theirs, tokens, gain, *after)


def norm_backward_kernel(after, values_ref, gain_ref, own_ref, got_ref, base_ref, *refs):
    outs = refs[after:]
    values = values_ref[...].astype(F32)
    grads = own_ref[...] + got_ref[...].astype(F32)
    scale = lax.rsqrt(jnp.mean(values * values, axis=-1, keepdims=True) + EPSILON)
    weighted = grads * gain_ref[...]
    scaled = values * scale
    inner = jnp.mean(scaled * weighted, axis=-1, keepdims=True)
    total = base_ref[...].astype(F32) + scale * (weighted - scaled * inner)
    for out in outs[1:]:
        out[...] = total.astype(out.dtype)

    @pl.when(pl.program_id(0) == 0)
    def _():
        outs[0][...] = jnp.zeros(outs[0].shape, F32)

    outs[0][...] += jnp.sum(grads * scaled, axis=0, keepdims=True)


def norm_backward(values, gain, own, got, base, dtypes, after):
    rows, depth = values.shape
    block = pl.BlockSpec((TILE, depth), lambda i: (i, 0))
    line = pl.BlockSpec((1, depth), lambda i: (0, 0))
    return pl.pallas_call(
        functools.partial(norm_backward_kernel, len(after)),
        grid=(rows // TILE,),
        in_specs=[block, line, block, block, block]
        + [pl.BlockSpec(memory_space=pl.ANY)] * len(after),
        out_specs=[line] + [block] * len(dtypes),
        out_shape=[jax.ShapeDtypeStruct((1, depth), F32)]
        + [jax.ShapeDtypeStruct((rows, depth), dtype) for dtype in dtypes],
        cost_estimate=cost(4, 0),
        name="norm_backward",
    )(values, gain, own, got, base, *after)


def finish_kernel(kept_ref, got_ref, *refs):
    outs, lines = refs[:-1], refs[-1]
    local = kept_ref.shape[0]
    width = outs[0].shape[1]
    heads = width // HEAD
    total = kept_ref[...] + got_ref[...].astype(F32)
    for place in range(4):
        outs[place][...] = total[:, place * width : (place + 1) * width]
    outs[4][...] = total[:, 4 * width : 5 * width].T
    for row in range(2):
        for h in range(heads):
            at = row * heads + h
            outs[5][row : row + 1, h * HEAD : (h + 1) * HEAD] = total[
                at : at + 1, 5 * width + HEAD :
            ]
    lines[...] = total[:, 5 * width : 5 * width + HEAD]
    for h in range(heads):
        outs[6][h * HEAD : (h + 1) * HEAD, :] = lines[pl.ds(h, local // heads, stride=heads), :].T


def finish(kept, got, width):
    local = kept.shape[0]
    heads = width // HEAD
    return pl.pallas_call(
        finish_kernel,
        out_shape=[jax.ShapeDtypeStruct((local, width), F32)] * 4
        + [
            jax.ShapeDtypeStruct((width, local), F32),
            jax.ShapeDtypeStruct((2, width), F32),
            jax.ShapeDtypeStruct((width, local // heads), F32),
        ],
        scratch_shapes=[pltpu.VMEM((local, HEAD), F32)],
        cost_estimate=cost(3, 0),
        name="finish",
    )(kept, got)


def open_grads_kernel(halves, half_tiles, passed, after, rank_ref, *refs):
    grads = refs[0][...].astype(F32)
    if halves == 2:
        mine = pl.program_id(0) // half_tiles == rank_ref[0]
        grads = jnp.where(mine, grads, refs[1][...].astype(F32))
    gate_ref, recalled_ref = refs[halves : halves + 2]
    attended_out, gate_out, recalled_out = refs[
        halves + 2 + passed + after : halves + 5 + passed + after
    ]
    opened = sigmoid(gate_ref[...])
    through = grads * opened
    attended_out[...] = grads.astype(BF16)
    recalled_out[...] = through.astype(BF16)
    gate_out[...] = (through * recalled_ref[...] * (1.0 - opened)).astype(BF16)


def chunk_map(place, half_tiles, halves):
    def index(i, rank_ref):
        start = (rank_ref[0] if place == 0 else 1 - rank_ref[0]) * half_tiles
        return jnp.clip(i - start, 0, half_tiles - 1), 0

    return index if halves == 2 else lambda i, rank_ref: (i, 0)


def open_grads(rank, chunks, gate_pre, recalled, passed, after):
    halves = len(chunks)
    rows, width = gate_pre.shape
    half_tiles = chunks[0].shape[0] // TILE
    block = pl.BlockSpec((TILE, width), lambda i, rank_ref: (i, 0))
    anywhere = pl.BlockSpec(memory_space=pl.ANY)
    shape = jax.ShapeDtypeStruct((rows, width), BF16)
    first = 1 + halves + 2
    return pl.pallas_call(
        functools.partial(open_grads_kernel, halves, half_tiles, len(passed), len(after)),
        grid_spec=pltpu.PrefetchScalarGridSpec(
            num_scalar_prefetch=1,
            grid=(rows // TILE,),
            in_specs=[
                pl.BlockSpec((TILE, width), chunk_map(place, half_tiles, halves))
                for place in range(halves)
            ]
            + [block] * 2
            + [anywhere] * (len(passed) + len(after)),
            out_specs=[block] * 3 + [anywhere] * len(passed),
        ),
        out_shape=[shape] * 3 + [jax.ShapeDtypeStruct(x.shape, x.dtype) for x in passed],
        input_output_aliases={first + i: 3 + i for i in range(len(passed))},
        cost_estimate=cost(3, 0),
        name="open_grads",
    )(rank.reshape(1), *chunks, gate_pre, recalled, *passed, *after)


class Group:
    def __init__(self):
        self.size = lax.axis_size("tp")
        self.rank = lax.axis_index("tp")

    def swap(self, values):
        return lax.ppermute(values, "tp", [(0, 1), (1, 0)])

    def spread(self, own):
        if self.size == 2:
            return [own, self.swap(own)]
        return [lax.all_gather(own, "tp", axis=0, tiled=True)]

    def collect(self, chunks):
        if self.size == 2:
            other = self.swap(chunks[1].astype(BF16))
            return chunks[0] + other.astype(F32)
        return lax.psum_scatter(
            chunks[0].astype(BF16), "tp", scatter_dimension=0, tiled=True
        ).astype(F32)

    def ordered(self, chunks):
        if self.size == 2:
            own, other = chunks
            first = self.rank == 0
            return jnp.concatenate(
                [jnp.where(first, own, other), jnp.where(first, other, own)], axis=0
            )
        return chunks[0]

    def chunks(self, rows):
        if self.size == 2:
            half = rows.shape[0] // 2
            return [
                lax.dynamic_slice_in_dim(rows, self.rank * half, half),
                lax.dynamic_slice_in_dim(rows, (1 - self.rank) * half, half),
            ]
        return [rows]


def gather_packed(parts):
    local = parts[0].shape[0]
    flat = [part.reshape(local, -1) for part in parts]
    widths = [part.shape[1] for part in flat]
    spare = -sum(widths) % 128
    if spare:
        flat.append(jnp.zeros((local, spare), flat[0].dtype))
    return lax.all_gather(jnp.concatenate(flat, axis=1), "fsdp", axis=0, tiled=True)


def gather_one(values):
    return lax.all_gather(values, "fsdp", axis=0, tiled=True)


CORES = [(i, i ^ 1) for i in range(16)]
PAIRS = [(i, i ^ 2) for i in range(16)]
AROUND = [(i, (i + 4) % 16) for i in range(16)]


def ring_gather(shard):
    place = lax.axis_index("fsdp")
    pieces, owners = [], []
    held = shard
    for step in range(4):
        owner = (place + 16 - 4 * step) % 16
        across = lax.ppermute(held, "fsdp", PAIRS)
        for piece, number in ((held, owner), (across, owner ^ 2)):
            pieces += [piece, lax.ppermute(piece, "fsdp", CORES)]
            owners += [number, number ^ 1]
        if step < 3:
            held = lax.ppermute(held, "fsdp", AROUND)
    return pieces, jnp.stack(owners)


def ring_scatter(mine, theirs):
    place = lax.axis_index("fsdp")
    y, z = (place // 2) % 2, place // 4
    got = lax.ppermute(theirs, "fsdp", CORES)

    def part(step, row):
        at = ((z + 3 - step) % 4) * 2 + row
        return lax.dynamic_index_in_dim(mine, at, 0, keepdims=False).astype(
            F32
        ) + lax.dynamic_index_in_dim(got, at, 0, keepdims=False).astype(F32)

    passed = []
    for step in range(4):
        other = part(step, 1 - y).astype(BF16)
        keep = part(step, y) + lax.ppermute(other, "fsdp", PAIRS).astype(F32)
        if step == 3:
            return keep, passed[-1], passed
        total = keep + passed[-1].astype(F32) if passed else keep
        passed.append(lax.ppermute(total.astype(BF16), "fsdp", AROUND))


def split_columns(values, widths):
    outs, at = [], 0
    for size in widths:
        outs.append(values[:, at : at + size])
        at += size
    return outs


def on_device(
    tokens,
    norm_gains,
    query_weight,
    key_weight,
    value_weight,
    mix_gate_weight,
    output_weight,
    persistent_tokens,
    memory_init,
    gate_weight,
    up_weight,
    down_weight,
    doc_ids,
    span_starts,
    memory_rates,
    out_grad,
):
    group = Group()
    fsdp = lax.axis_size("fsdp")
    local, width = query_weight.shape
    depth = fsdp * local
    special = group.size == 2 and fsdp == 16 and depth == 4 * TILE
    token_chunks = group.spread(tokens)
    grad_chunks = group.spread(out_grad)
    if special:
        pieces, owners = ring_gather(
            pack_first(
                query_weight, key_weight, value_weight, mix_gate_weight, memory_init,
                persistent_tokens, norm_gains,
            )
        )
        (
            packed, normed_all, queries, key_rows, value_rows, gate_pre, gains, persist, init
        ) = project_pieces(
            jnp.concatenate([owners * local, group.rank.reshape(1)]).astype(jnp.int32),
            token_chunks, pieces, width,
        )
        seconds = [output_weight.T, group.swap(output_weight.T)]
    else:
        packed = gather_packed(
            [
                query_weight,
                key_weight,
                value_weight,
                mix_gate_weight,
                memory_init.T.reshape(local, -1),
                persistent_tokens.reshape(local, -1),
                norm_gains.T,
            ]
        )
        spots = [
            4 * width,
            4 * width + 2 * HEAD * width // depth,
            4 * width + (2 * HEAD + 2 * PERSIST) * width // depth,
        ]
        init = packed[:, spots[0] : spots[1]].reshape(2 * HEAD, width).T.astype(F32)
        persist = packed[:, spots[1] : spots[2]].reshape(2 * PERSIST, width)
        gains = packed[:, spots[2] : spots[2] + 2].T.astype(F32)
        normed_all, queries, key_rows, value_rows, gate_pre = project(
            group.rank, gains[0], token_chunks, packed, width
        )
        seconds = [output_weight.T]
    w_out, *w_out_other, w_gate, w_up, w_down = split_columns(
        gather_packed(seconds + [gate_weight, up_weight, down_weight.T]),
        [width] * len(seconds) + [gate_weight.shape[1]] * 3,
    )

    rows_in = tokens.astype(F32)
    doc_blocks = doc_ids.reshape(-1, SPAN)
    live = (doc_blocks == doc_blocks[:, SPAN - 1 :]).astype(F32) / SPAN
    recalled, states = memory_forward(
        queries, key_rows, value_rows, live, span_starts, memory_rates, init
    )
    combined, logs = attention_forward(
        queries, key_rows, value_rows, persist, doc_ids, gate_pre, recalled, grad_chunks[-1]
    )
    half = tokens.shape[0]
    base = (group.rank * (half // TILE)).astype(jnp.int32)
    hidden_grads = [matmul(grads, w_down) for grads in grad_chunks]
    if special:
        got = group.swap(group.chunks(combined)[1])
        hidden_one, normed_two = branch_norm(
            base.reshape(1), combined, got, w_out, w_out_other[0], tokens, gains[1:2], hidden_grads
        )
    else:
        branch = group.collect([matmul_right(chunk, w_out) for chunk in group.chunks(combined)])
        hidden_one = rows_in + branch
        normed_two = rms_norm(hidden_one, gains[1]).astype(BF16)
    normed_chunks = group.spread(normed_two)

    ffn, back_chunks, gate_backs, up_backs, hiddens = [], [], [], [], []
    for rows, hidden_grad in zip(normed_chunks, hidden_grads):
        gate_rows = matmul(rows, w_gate)
        up_rows = matmul(rows, w_up)
        gate_sigmoid = jax.nn.sigmoid(gate_rows)
        hidden = (gate_rows * gate_sigmoid * up_rows).astype(BF16)
        gate_back = (
            hidden_grad * up_rows * gate_sigmoid * (1.0 + gate_rows * (1.0 - gate_sigmoid))
        ).astype(BF16)
        up_back = (hidden_grad * gate_rows * gate_sigmoid).astype(BF16)
        ffn.append(matmul_right(hidden, w_down))
        back_chunks.append(matmul_right(gate_back, w_gate) + matmul_right(up_back, w_up))
        hiddens.append(hidden)
        gate_backs.append(gate_back)
        up_backs.append(up_back)
    if special:
        back_other = group.swap(back_chunks[1].astype(BF16))
    groups = [(normed_chunks, [gate_backs, up_backs]), (grad_chunks, [hiddens])]
    if gate_weight.shape[1] % 128:
        ffn_grads = jnp.concatenate(
            [
                sum(turn(*pair) for pair in zip(lefts, right)).astype(BF16)
                for lefts, rights in groups
                for right in rights
            ],
            axis=1,
        )
    else:
        ffn_grads = weight_grads(groups)
    ffn_sums = lax.psum_scatter(ffn_grads, "fsdp", scatter_dimension=0, tiled=True)
    if special:
        gain_two_grad, hidden_one_grad, branch_own = norm_backward(
            hidden_one, gains[1:2], back_chunks[0], back_other, out_grad, [F32, BF16], []
        )
        combined_grads = [
            matmul(branch_own, w_out),
            group.swap(matmul(branch_own, w_out_other[0]).astype(BF16)),
        ]
        attended_grad, gate_pre_grad, recalled_grad, branch_own, ffn_other = open_grads(
            group.rank, combined_grads, gate_pre, recalled,
            [branch_own, ffn[1].astype(BF16)], [ffn_grads],
        )
        branch_rows = group.ordered([branch_own, group.swap(branch_own)])
        ffn = [ffn[0], ffn_other]
    else:
        inner_grad, gain_two_grad = norm_back(
            hidden_one, gains[1], group.collect(back_chunks)
        )
        hidden_one_grad = out_grad.astype(F32) + inner_grad
        branch_rows = group.ordered(group.spread(hidden_one_grad.astype(BF16)))
        attended_grad, gate_pre_grad, recalled_grad = open_grads(
            group.rank, [matmul(branch_rows, w_out)], gate_pre, recalled, [], []
        )
    output = (hidden_one + group.collect(ffn)).astype(BF16)
    query_mem, key_mem, value_mem, init_grad = memory_backward(
        queries, key_rows, value_rows, live, span_starts, memory_rates, recalled_grad, states
    )
    query_back, key_back, value_back, persist_grad = attention_backward(
        queries, key_rows, value_rows, persist, doc_ids, logs, attended_grad,
        query_mem, key_mem, value_mem,
    )
    backs = [query_back, key_back, value_back, gate_pre_grad]
    pairs = [([normed_all], [[back] for back in backs]), ([branch_rows], [[combined]])]
    if special:
        kept, got, passed = ring_scatter(
            *weight_grads(pairs, [init_grad, persist_grad], lax.axis_index("fsdp") % 2)
        )
        query_out, key_out, value_out, mix_out, out_weight_out, persist_out, init_out = finish(
            kept, got, width
        )
        other = project_back(half // TILE - base, half, backs, packed, BF16)
        own = project_back(base, half, backs, packed, F32)
        gain_one_grad, tokens_grad = norm_backward(
            tokens, gains[0:1], own, group.swap(other), hidden_one_grad, [BF16], [passed[1]]
        )
    else:
        small = [init_grad.reshape(depth, -1), persist_grad.reshape(depth, -1)]
        widths = [width] * 5 + [piece.shape[1] for piece in small]
        spare = -sum(widths) % 128
        small = jnp.concatenate(small + [jnp.zeros((depth, spare), F32)], axis=1).astype(BF16)
        sums = lax.psum_scatter(
            weight_grads(pairs, [small]), "fsdp", scatter_dimension=0, tiled=True
        ).astype(F32)
        (
            query_out, key_out, value_out, mix_out, out_weight_out, init_out, persist_out
        ) = split_columns(sums, widths)
        out_weight_out = out_weight_out.T
        persist_out = persist_out.reshape(persistent_tokens.shape)
        init_out = init_out.reshape(-1, width).T
        normed_grad = group.collect(
            [project_back(jnp.int32(0), half * group.size, backs, packed, BF16)]
        )
        input_grad, gain_one_grad = norm_back(rows_in, gains[0], normed_grad)
        tokens_grad = (hidden_one_grad + input_grad).astype(BF16)
    gate_out, up_out, down_out = split_columns(
        ffn_sums.astype(F32), [gate_weight.shape[1]] * 3
    )
    gain_terms = jnp.stack([gain_one_grad, gain_two_grad]).reshape(2, fsdp, local)
    gain_terms = lax.all_to_all(gain_terms.transpose(1, 0, 2), "fsdp", 0, 0, tiled=True)
    gains_grad = lax.psum(jnp.sum(gain_terms, axis=0), "tp")
    return (
        output,
        tokens_grad,
        gains_grad,
        query_out,
        key_out,
        value_out,
        mix_out,
        out_weight_out,
        persist_out,
        init_out,
        gate_out,
        up_out,
        down_out.T,
    )


def solution(mesh):
    placed = (
        P(("fsdp", "tp"), None),
        P(None, "fsdp"),
        P("fsdp", "tp"),
        P("fsdp", "tp"),
        P("fsdp", "tp"),
        P("fsdp", "tp"),
        P("tp", "fsdp"),
        P("fsdp", "tp"),
        P("tp", "fsdp"),
        P("fsdp", "tp"),
        P("fsdp", "tp"),
        P("tp", "fsdp"),
        P("fsdp"),
        P("fsdp"),
        P(None, "fsdp", "tp"),
        P(("fsdp", "tp"), None),
    )
    return jax.shard_map(
        on_device,
        mesh=mesh,
        in_specs=placed,
        out_specs=(
            P(("fsdp", "tp"), None),
            P(("fsdp", "tp"), None),
            P(None, "fsdp"),
            P("fsdp", "tp"),
            P("fsdp", "tp"),
            P("fsdp", "tp"),
            P("fsdp", "tp"),
            P("tp", "fsdp"),
            P("fsdp", "tp"),
            P("tp", "fsdp"),
            P("fsdp", "tp"),
            P("fsdp", "tp"),
            P("tp", "fsdp"),
        ),
        check_vma=False,
    )
```
